128 devices in a mesh: row: 8 (over y, z_lo), col: 16 (over x, z_hi, core).
Axes of the slice: x: 4, y: 4, z: 4 (z_hi: 2, z_lo: 2; z = z_hi * 2 + z_lo), core: 2. Of those that a mesh axis runs over, the one named last changes fastest.
Arguments:
- pair_state: bfloat16 [384, 384, 128], P('row', 'col'), may hold values from -6 to 6
- tile_mask: int32 [3, 3], replicated, may hold values from 0 to 1, as said below
- weight_in: bfloat16 [2, 128, 640], replicated, may hold values from -0.5 to 0.5
- weight_out: bfloat16 [2, 128, 128], replicated, may hold values from -0.5 to 0.5
- gain_in: float32 [2, 128], replicated, may hold values from 0.1 to 1.9
- gain_out: float32 [2, 128], replicated, may hold values from 0.1 to 1.9
- cotangent: bfloat16 [384, 384, 128], P('row', 'col'), may hold values from -6 to 6
Outputs:
- updated_pair: bfloat16 [384, 384, 128], P('row', 'col')
- pair_grad: float32 [384, 384, 128], P('row', 'col')
The draws below stay inside these ranges and needn't reach their ends.
Inputs may be any that keep to these rules, and one draw needn't show every extreme that they name: `tile_mask`: Symmetric. The tiles form runs of consecutive chains, at least two; every tile pair inside one chain is 1, and all tile pairs of one pair of chains share one value.
All inputs are finite; a program needn't handle non-finite values.
Results may differ from the reference program's by a relative error of at most 0.012.
Values may be sent and summed in bfloat16 or wider, within the bound.
No kernel may reach another device: no remote copies, remote signals or barrier semaphores. Data moves between devices by JAX's collectives and lax.ppermute only.
A program may use at most 128 MiB of HBM per device.

```python
import jax
import jax.numpy as jnp
from jax import lax

CH = 128
HID = 128
RES = 384
TILES = 3


def draw_tile_mask(key, part):
    base = jax.random.fold_in(key, 7)
    key_breaks, key_forced, key_active = jax.random.split(base, 3)
    positions = jnp.arange(TILES, dtype=jnp.int32)
    breaks = jax.random.randint(key_breaks, (TILES,), 0, 2).astype(jnp.int32)
    forced = jax.random.randint(key_forced, (), 1, TILES).astype(jnp.int32)
    breaks = jnp.where(positions == forced, 1, breaks)
    breaks = breaks * (positions > 0).astype(jnp.int32)
    chain_of_tile = jnp.cumsum(breaks).astype(jnp.int32)
    active = (jax.random.randint(key_active, (TILES, TILES), 0, 10) < 3).astype(jnp.int32)
    upper = jnp.triu(active, 1)
    active = upper + upper.T + jnp.eye(TILES, dtype=jnp.int32)
    return active[chain_of_tile][:, chain_of_tile].astype(jnp.int32)


def block_levels(key, shape, cuts, least, top_value):
    gain = 1.0
    for dim, shards_of in cuts:
        heights = jax.random.uniform(jax.random.fold_in(jax.random.fold_in(key, 6), dim), (shards_of,), jnp.float32, least / len(cuts), top_value / len(cuts))
        gain = gain * jnp.repeat(jnp.exp(heights), shape[dim] // shards_of).reshape((-1,) + (1,) * (len(shape) - 1 - dim))
    return gain


def bell_draw(own_key, shape, deviation, limit, cuts=(), held_as=jnp.bfloat16):
    values = deviation * jax.random.normal(own_key, shape, jnp.float32)
    if cuts:
        values = values * block_levels(own_key, shape, cuts, -0.22, 0.18)
    return jnp.clip(values, -limit, limit).astype(held_as)


def setup_inputs(seed: int = 0) -> dict:
    streams_of = jax.random.split(jax.random.key(seed), 8)
    pair_state = bell_draw(streams_of[0], (RES, RES, CH), 1.0, 6.0, ((0, 8), (1, 16)))
    tile_mask = draw_tile_mask(jax.random.fold_in(streams_of[7], 71), 0)
    weight_in = bell_draw(streams_of[2], (2, CH, 4 * HID + CH), CH ** -0.5, 0.5)
    weight_out = bell_draw(streams_of[3], (2, HID, CH), HID ** -0.5, 0.5)
    gain_in = jnp.clip(1.0 + 0.18 * jax.random.normal(streams_of[4], (2, CH), jnp.float32), 0.1, 1.9)
    gain_out = jnp.clip(1.0 + 0.18 * jax.random.normal(streams_of[5], (2, HID), jnp.float32), 0.1, 1.9)
    cotangent = bell_draw(streams_of[6], (RES, RES, CH), 1.0, 6.0, ((0, 8), (1, 16)))
    return dict(pair_state=pair_state, tile_mask=tile_mask, weight_in=weight_in, weight_out=weight_out, gain_in=gain_in, gain_out=gain_out, cotangent=cotangent)


norm_eps = 1e-05

def normalize(values):
    center = values - lax.optimization_barrier(jnp.mean(values, axis=-1, keepdims=True))
    inv_scale = lax.rsqrt(lax.optimization_barrier(jnp.mean(center * center, axis=-1, keepdims=True)) + norm_eps)
    return (center * inv_scale, inv_scale)

def norm_back(standard, inv_scale, gain_vec, upstream):
    scaled = upstream * gain_vec
    return inv_scale * (scaled - lax.optimization_barrier(jnp.mean(scaled, axis=-1, keepdims=True)) - standard * lax.optimization_barrier(jnp.mean(scaled * standard, axis=-1, keepdims=True)))

def project(pair_in, tile_gate, weight_layer, gain_vec):
    standard, inv_scale = normalize(pair_in.astype(jnp.float32))
    normed = (standard * gain_vec).astype(jnp.bfloat16)
    channels = pair_in.shape[-1]
    hidden = (weight_layer.shape[1] - channels) // 4
    projected = jnp.dot(normed.reshape(-1, channels), weight_layer, preferred_element_type=jnp.float32)
    projected = projected.reshape(pair_in.shape[:-1] + (weight_layer.shape[1],))
    gate_col = tile_gate[..., None]
    left_side = (gate_col * jax.nn.sigmoid(projected[..., hidden:2 * hidden]) * projected[..., :hidden]).astype(jnp.bfloat16)
    right_side = (gate_col * jax.nn.sigmoid(projected[..., 3 * hidden:4 * hidden]) * projected[..., 2 * hidden:3 * hidden]).astype(jnp.bfloat16)
    return (standard, inv_scale, projected, left_side, right_side)

def finish(pair_in, inner_sum, projected, tile_gate, weight_layer, gain_vec):
    standard, inv_scale = normalize(inner_sum)
    normed = (standard * gain_vec).astype(jnp.bfloat16)
    hidden = inner_sum.shape[-1]
    update = jnp.dot(normed.reshape(-1, hidden), weight_layer, preferred_element_type=jnp.float32).reshape(pair_in.shape)
    gate_sig = jax.nn.sigmoid(projected[..., 4 * hidden:])
    result = (pair_in.astype(jnp.float32) + tile_gate[..., None] * gate_sig * update).astype(jnp.bfloat16)
    return (result, (standard, inv_scale, update))

def back_top(upstream, projected, tile_gate, saved, weight_layer, gain_vec):
    standard, inv_scale, update = saved
    hidden = weight_layer.shape[0]
    channels = weight_layer.shape[1]
    gate_sig = jax.nn.sigmoid(projected[..., 4 * hidden:])
    gated_grad = upstream * tile_gate[..., None]
    d_update = (gated_grad * gate_sig).astype(jnp.bfloat16)
    d_outgate = gated_grad * update * gate_sig * (1.0 - gate_sig)
    d_normed = jnp.dot(d_update.reshape(-1, channels), weight_layer.T, preferred_element_type=jnp.float32).reshape(standard.shape)
    d_inner = norm_back(standard, inv_scale, gain_vec, d_normed).astype(jnp.bfloat16)
    return (d_inner, d_outgate)

def back_bottom(upstream, d_left, d_right, d_outgate, projected, tile_gate, standard, inv_scale, weight_layer, gain_vec):
    hidden = d_left.shape[-1]
    gate_col = tile_gate[..., None]
    left_sig = jax.nn.sigmoid(projected[..., hidden:2 * hidden])
    right_sig = jax.nn.sigmoid(projected[..., 3 * hidden:4 * hidden])
    pieces = [d_left * gate_col * left_sig, d_left * gate_col * projected[..., :hidden] * left_sig * (1.0 - left_sig), d_right * gate_col * right_sig, d_right * gate_col * projected[..., 2 * hidden:3 * hidden] * right_sig * (1.0 - right_sig), d_outgate]
    d_proj = jnp.concatenate(pieces, axis=-1).astype(jnp.bfloat16)
    d_normed = jnp.dot(d_proj.reshape(-1, d_proj.shape[-1]), weight_layer.T, preferred_element_type=jnp.float32).reshape(standard.shape)
    return upstream + norm_back(standard, inv_scale, gain_vec, d_normed)

def reference(pair_state, tile_mask, weight_in, weight_out, gain_in, gain_out, cotangent):
    tile_width = RES // TILES
    tile_ids = jnp.arange(RES, dtype=jnp.int32) // tile_width
    onehot = (tile_ids[:, None] == jnp.arange(TILES, dtype=jnp.int32)[None, :]).astype(jnp.float32)
    tile_gate = jnp.dot(jnp.dot(onehot, tile_mask.astype(jnp.float32), precision=lax.Precision.HIGHEST), onehot.T, precision=lax.Precision.HIGHEST)
    front = project(pair_state, tile_gate, weight_in[0], gain_in[0])
    left_front = front[3].astype(jnp.float32)
    right_front = front[4].astype(jnp.float32)
    inner_front = jnp.einsum('ikh,jkh->ijh', left_front, right_front)
    middle_pair, top_front = finish(pair_state, inner_front, front[2], tile_gate, weight_out[0], gain_out[0])
    second = project(middle_pair, tile_gate, weight_in[1], gain_in[1])
    left_second = second[3].astype(jnp.float32)
    right_second = second[4].astype(jnp.float32)
    inner_second = jnp.einsum('kih,kjh->ijh', left_second, right_second)
    updated_pair, top_second = finish(middle_pair, inner_second, second[2], tile_gate, weight_out[1], gain_out[1])
    grad_last = cotangent.astype(jnp.float32)
    d_inner_second, d_gate_second = back_top(grad_last, second[2], tile_gate, top_second, weight_out[1], gain_out[1])
    grad_second = d_inner_second.astype(jnp.float32)
    d_left_second = jnp.einsum('kjh,ijh->kih', right_second, grad_second)
    d_right_second = jnp.einsum('kih,ijh->kjh', left_second, grad_second)
    grad_middle = back_bottom(grad_last, d_left_second, d_right_second, d_gate_second, second[2], tile_gate, second[0], second[1], weight_in[1], gain_in[1])
    d_inner_front, d_gate_front = back_top(grad_middle, front[2], tile_gate, top_front, weight_out[0], gain_out[0])
    grad_front = d_inner_front.astype(jnp.float32)
    d_left_front = jnp.einsum('ijh,jkh->ikh', grad_front, right_front)
    d_right_front = jnp.einsum('ijh,ikh->jkh', grad_front, left_front)
    pair_grad = back_bottom(grad_middle, d_left_front, d_right_front, d_gate_front, front[2], tile_gate, front[0], front[1], weight_in[0], gain_in[0])
    return (updated_pair, pair_grad)
```

```python
import functools

import jax
import jax.numpy as jnp
from jax import lax
from jax.experimental import pallas as pl
from jax.experimental.pallas import tpu as pltpu
from jax.sharding import PartitionSpec as P

RES = 384
TILES = 3
TILE = RES // TILES
CH = 128
ROWS = 8
COLS = 16
A = RES // ROWS
B = RES // COLS
PAIRS = A * B
NB = 8
CHUNK = NB * A
F32 = jnp.float32
BF16 = jnp.bfloat16
EPS = 1e-05
AXES = ("row", "col")
VM = pl.BlockSpec(memory_space=pltpu.VMEM)
SM = pl.BlockSpec(memory_space=pltpu.SMEM)


def normalize(values):
    center = values - jnp.mean(values, axis=-1, keepdims=True)
    inv = lax.rsqrt(jnp.mean(center * center, axis=-1, keepdims=True) + EPS)
    return center * inv, inv


def norm_back(standard, inv, gain, upstream):
    scaled = upstream * gain
    return inv * (
        scaled
        - jnp.mean(scaled, axis=-1, keepdims=True)
        - standard * jnp.mean(scaled * standard, axis=-1, keepdims=True)
    )


def mm(x, w):
    return lax.dot_general(x, w, (((1,), (0,)), ((), ())), preferred_element_type=F32)


def mm_nt(x, w):
    return lax.dot_general(x, w, (((1,), (1,)), ((), ())), preferred_element_type=F32)


def mm_tn(x, w):
    return lax.dot_general(x, w, (((0,), (0,)), ((), ())), preferred_element_type=F32)


def gate_chunk(mask_ref, b0):
    row_first = lax.axis_index("row") * A
    col_first = lax.axis_index("col") * B
    t0 = row_first // TILE
    t1 = jnp.minimum(t0 + 1, TILES - 1)
    low = lax.broadcasted_iota(jnp.int32, (A, CH), 0) < (t0 + 1) * TILE - row_first
    parts = []
    for k in range(NB):
        jt = (col_first + b0 + k) // TILE
        m0 = mask_ref[t0, jt].astype(F32)
        m1 = mask_ref[t1, jt].astype(F32)
        parts.append(jnp.where(low, jnp.full((A, CH), m0, F32), jnp.full((A, CH), m1, F32)))
    return jnp.concatenate(parts, axis=0)


def rows_of(chunk):
    return pl.ds(pl.multiple_of(chunk * CHUNK, CHUNK), CHUNK)


def load_turned(ref, b0):
    return jnp.concatenate([ref[pl.ds(b0 + k, A, stride=B), :] for k in range(NB)], axis=0)


def store_turned(ref, b0, value):
    for k in range(NB):
        ref[pl.ds(b0 + k, A, stride=B), :] = value[k * A:(k + 1) * A]


def pack_two(ref, b0, left, right):
    fill = jnp.zeros((CH - 2 * A, CH), F32)
    for k in range(NB):
        block = jnp.concatenate(
            [left[k * A:(k + 1) * A], right[k * A:(k + 1) * A], fill], axis=0
        )
        ref[pl.ds(b0 + k, CH, stride=B), :] = jnp.transpose(block)


def pack_one(ref, src):
    for b in range(16):
        first = src[pl.ds(b * A, A), :]
        if b < 8:
            second = src[pl.ds((b + 16) * A, A), :]
        else:
            second = jnp.zeros((A, CH), F32)
        block = jnp.concatenate([first, second, jnp.zeros((CH - 2 * A, CH), F32)], axis=0)
        ref[pl.ds(b, CH, stride=16), :] = jnp.transpose(block)


def unpack_one(msg_ref, wide, dst):
    wide[...] = msg_ref[...].astype(F32)
    for b in range(16):
        block = jnp.transpose(wide[pl.ds(b, CH, stride=16), :])
        dst[pl.ds(b * A, A), :] = block[:A]
        if b < 8:
            dst[pl.ds((b + 16) * A, A), :] = block[A:2 * A]


def unpack_two(wide, b0):
    lefts, rights = [], []
    for k in range(NB):
        block = jnp.transpose(wide[pl.ds(b0 + k, CH, stride=B), :])
        lefts.append(block[:A])
        rights.append(block[A:2 * A])
    return jnp.concatenate(lefts, axis=0), jnp.concatenate(rights, axis=0)


def sides(gate, proj):
    left = gate * jax.nn.sigmoid(proj[:, CH:2 * CH]) * proj[:, :CH]
    right = gate * jax.nn.sigmoid(proj[:, 3 * CH:4 * CH]) * proj[:, 2 * CH:3 * CH]
    return left, right


def chunks(fn):
    def step(i, carry):
        fn(i, i * NB)
        return carry

    lax.fori_loop(0, B // NB, step, 0)


def k_first(mask_ref, pair_ref, win_ref, gin_ref, msg_ref, x_ref, normed_ref, wide, msgf):
    wide[...] = pair_ref[...].astype(F32)

    def chunk(i, b0):
        gate = gate_chunk(mask_ref, b0)
        x = load_turned(wide, b0)
        x_ref[rows_of(i), :] = x.astype(BF16)
        standard, _ = normalize(x)
        normed = (standard * gin_ref[0:1, :]).astype(BF16)
        normed_ref[rows_of(i), :] = normed
        proj = mm(normed, win_ref[0, :, :4 * CH])
        left, right = sides(gate, proj)
        pack_two(msgf, b0, left, right)

    chunks(chunk)
    msg_ref[...] = msgf[...].astype(BF16)


def k_second(
    mask_ref, in_ref, x_ref, normed_ref, win_ref, wout_ref, gin_ref, gout_ref,
    msg_ref, inner_ref, mid_ref, normed1_ref, wide, inner, msgf,
):
    unpack_one(in_ref, wide, inner)

    def chunk(i, b0):
        gate = gate_chunk(mask_ref, b0)
        rows = rows_of(i)
        value = inner[rows, :]
        inner_ref[rows, :] = value.astype(BF16)
        standard, _ = normalize(value)
        update = mm((standard * gout_ref[0:1, :]).astype(BF16), wout_ref[0])
        sig = jax.nn.sigmoid(mm(normed_ref[rows, :], win_ref[0, :, 4 * CH:]))
        middle = (x_ref[rows, :].astype(F32) + gate * sig * update).astype(BF16)
        mid_ref[rows, :] = middle
        standard, _ = normalize(middle.astype(F32))
        normed = (standard * gin_ref[1:2, :]).astype(BF16)
        normed1_ref[rows, :] = normed
        left, right = sides(gate, mm(normed, win_ref[1, :, :4 * CH]))
        pack_two(msgf, b0, left, right)

    chunks(chunk)
    msg_ref[...] = msgf[...].astype(BF16)


def top_back(upstream, gate, normed, inner_value, u, win_ref, wout_ref, gout_ref):
    sig = jax.nn.sigmoid(mm(normed, win_ref[u, :, 4 * CH:]))
    gain = gout_ref[u:u + 1, :]
    standard, inv = normalize(inner_value)
    update = mm((standard * gain).astype(BF16), wout_ref[u])
    gated = upstream * gate
    d_update = (gated * sig).astype(BF16)
    d_gate = gated * update * sig * (1.0 - sig)
    d_inner = norm_back(standard, inv, gain, mm_nt(d_update, wout_ref[u]))
    return sig * update, d_gate, d_inner


def bottom_back(d_left, d_right, d_gate, gate, normed, state, u, win_ref, gin_ref):
    proj = mm(normed, win_ref[u, :, :4 * CH])
    left_sig = jax.nn.sigmoid(proj[:, CH:2 * CH])
    right_sig = jax.nn.sigmoid(proj[:, 3 * CH:4 * CH])
    d_left = d_left * gate * left_sig
    d_right = d_right * gate * right_sig
    d_proj = jnp.concatenate(
        [
            d_left.astype(BF16),
            (d_left * proj[:, :CH] * (1.0 - left_sig)).astype(BF16),
            d_right.astype(BF16),
            (d_right * proj[:, 2 * CH:3 * CH] * (1.0 - right_sig)).astype(BF16),
            d_gate,
        ],
        axis=1,
    )
    d_normed = mm_nt(d_proj, win_ref[u])
    standard, inv = normalize(state.astype(F32))
    return norm_back(standard, inv, gin_ref[u:u + 1, :], d_normed)


def k_third(
    mask_ref, in_ref, mid_ref, normed1_ref, cot_ref, win_ref, wout_ref, gout_ref,
    msg_ref, out_ref, cot_out_ref, dgate_ref, wide, inner, cotf, outf, msgf,
):
    unpack_one(in_ref, wide, inner)
    cotf[...] = cot_ref[...].astype(F32)

    def chunk(i, b0):
        gate = gate_chunk(mask_ref, b0)
        rows = rows_of(i)
        grad = load_turned(cotf, b0)
        cot_out_ref[rows, :] = grad.astype(BF16)
        gated_update, d_gate, d_inner = top_back(
            grad, gate, normed1_ref[rows, :], inner[rows, :], 1, win_ref, wout_ref, gout_ref
        )
        store_turned(outf, b0, mid_ref[rows, :].astype(F32) + gate * gated_update)
        dgate_ref[rows, :] = d_gate.astype(BF16)
        inner[rows, :] = d_inner

    chunks(chunk)
    out_ref[...] = outf[...].astype(BF16)
    pack_one(msgf, inner)
    msg_ref[...] = msgf[...].astype(BF16)


def k_fourth(
    mask_ref, in_ref, mid_ref, normed1_ref, cot_ref, dgate1_ref, inner0_ref, normed0_ref,
    win_ref, wout_ref, gin_ref, gout_ref,
    msg_ref, grad_ref, dgate_ref, wide, inner, msgf,
):
    wide[...] = in_ref[...].astype(F32)

    def chunk(i, b0):
        gate = gate_chunk(mask_ref, b0)
        rows = rows_of(i)
        d_left, d_right = unpack_two(wide, b0)
        grad = cot_ref[rows, :].astype(F32) + bottom_back(
            d_left, d_right, dgate1_ref[rows, :], gate, normed1_ref[rows, :], mid_ref[rows, :],
            1, win_ref, gin_ref,
        )
        grad_ref[rows, :] = grad
        _, d_gate, d_inner = top_back(
            grad, gate, normed0_ref[rows, :], inner0_ref[rows, :].astype(F32), 0,
            win_ref, wout_ref, gout_ref,
        )
        dgate_ref[rows, :] = d_gate.astype(BF16)
        inner[rows, :] = d_inner

    chunks(chunk)
    pack_one(msgf, inner)
    msg_ref[...] = msgf[...].astype(BF16)


def k_fifth(
    mask_ref, in_ref, x_ref, normed0_ref, grad_ref, dgate0_ref, win_ref, gin_ref,
    out_ref, wide,
):
    wide[...] = in_ref[...].astype(F32)

    def chunk(i, b0):
        gate = gate_chunk(mask_ref, b0)
        rows = rows_of(i)
        d_left, d_right = unpack_two(wide, b0)
        grad = grad_ref[rows, :] + bottom_back(
            d_left, d_right, dgate0_ref[rows, :], gate, normed0_ref[rows, :], x_ref[rows, :],
            0, win_ref, gin_ref,
        )
        store_turned(out_ref, b0, grad)

    chunks(chunk)


def lanes(n):
    return lax.broadcasted_iota(jnp.int32, (n, 128), 1)


def turn(value, shift):
    shift = shift % 128
    return value if shift == 0 else pltpu.roll(value, shift, axis=1)


def spread(pieces):
    lane = lanes(pieces[0].shape[0])
    tiles = []
    for t in range(3):
        inside = [r for r in range(ROWS) if r * A < (t + 1) * 128 and (r + 1) * A > t * 128]
        tile = pieces[inside[-1]]
        for r in reversed(inside[:-1]):
            tile = jnp.where(lane < (r + 1) * A - t * 128, pieces[r], tile)
        tiles.append(tile)
    return tiles


def cut(tiles, r, place):
    t, off = divmod(r * A, 128)
    if off + A <= 128:
        return turn(tiles[t], place - off)
    lane = lanes(tiles[t].shape[0])
    both = jnp.where(lane >= off, tiles[t], tiles[t + 1])
    return turn(both, place - off)


STEP = 48


def join_two(x_ref, lt, rt):
    for s in range(RES // STEP):
        blocks = [x_ref[r * RES + s * STEP:r * RES + (s + 1) * STEP, :].astype(F32) for r in range(ROWS)]
        for dst, start in ((lt, 0), (rt, A)):
            tiles = spread([turn(v, r * A - start) for r, v in enumerate(blocks)])
            for t in range(3):
                dst[s * STEP:(s + 1) * STEP, t * 128:(t + 1) * 128] = tiles[t].astype(BF16)


def join_one(x_ref, dst):
    for c in range(0, COLS, 2):
        rows = [[], [], []]
        for cc in (c, c + 1):
            blocks = [x_ref[(r * COLS + cc) * 16:(r * COLS + cc) * 16 + 16, :].astype(F32) for r in range(ROWS)]
            top = spread([turn(v, r * A) for r, v in enumerate(blocks)])
            end = spread([turn(v[:8], r * A - A) for r, v in enumerate(blocks)])
            for t in range(3):
                rows[t] += [top[t], end[t]]
        for t in range(3):
            dst[c * B:(c + 2) * B, t * 128:(t + 1) * 128] = jnp.concatenate(rows[t], axis=0).astype(BF16)


def split_two(lt, rt, o_ref):
    for s in range(RES // STEP):
        rows = slice(s * STEP, (s + 1) * STEP)
        left = [lt[rows, t * 128:(t + 1) * 128] for t in range(3)]
        right = [rt[rows, t * 128:(t + 1) * 128] for t in range(3)]
        lane = lanes(STEP)
        for r in range(ROWS):
            block = jnp.where(lane < A, cut(left, r, 0), cut(right, r, A))
            o_ref[r * RES + s * STEP:r * RES + (s + 1) * STEP, :] = block.astype(BF16)


def split_one(value, o_ref):
    for c in range(COLS):
        tiles = [value[c * B:(c + 1) * B, t * 128:(t + 1) * 128] for t in range(3)]
        lane = lanes(8)
        for r in range(ROWS):
            top = cut([v[:16] for v in tiles], r, 0)
            end = cut([v[16:] for v in tiles], r, A)
            block = jnp.concatenate([jnp.where(lane < A, top[:8], end), top[8:]], axis=0)
            o_ref[(r * COLS + c) * 16:(r * COLS + c) * 16 + 16, :] = block.astype(BF16)


def m_forward(u, x_ref, o_ref, lt, rt, prod):
    join_two(x_ref, lt, rt)
    if u == 0:
        prod[...] = mm_tn(rt[...], lt[...])
    else:
        prod[...] = mm_nt(rt[...], lt[...])
    split_one(prod, o_ref)


def m_backward(u, x_ref, lt, rt, o_ref, dt, prod_l, prod_r):
    join_one(x_ref, dt)
    if u == 0:
        prod_l[...] = mm(rt[...], dt[...])
        prod_r[...] = mm_nt(lt[...], dt[...])
    else:
        prod_l[...] = mm_tn(dt[...], rt[...])
        prod_r[...] = mm(dt[...], lt[...])
    split_two(prod_l, prod_r, o_ref)


def shape(*dims, dtype=BF16):
    return jax.ShapeDtypeStruct(dims, dtype)


def call(fn, outs, scratch, name, smem=True):
    def run(*args):
        specs = ([SM] if smem else []) + [VM] * (len(args) - (1 if smem else 0))
        return pl.pallas_call(
            fn,
            out_shape=outs,
            in_specs=specs,
            out_specs=[VM] * len(outs),
            scratch_shapes=scratch,
            compiler_params=pltpu.CompilerParams(vmem_limit_bytes=24 * 1024 * 1024),
            name=name,
        )(*args)

    return run


def exchange(message, rows):
    message = message.reshape(ROWS * COLS, rows, 128)
    return lax.all_to_all(message, AXES, 0, 0, tiled=True).reshape(ROWS * COLS * rows, 128)


TWO = (CH * B, 128)
ONE = (CH * 16, 128)
PAIR = (PAIRS, CH)
FULL = (RES, RES)


def wide(dims):
    return pltpu.VMEM(dims, F32)


def body(pair_state, tile_mask, weight_in, weight_out, gain_in, gain_out, cotangent):
    msg, x, normed0 = call(
        k_first, (shape(*TWO), shape(*PAIR), shape(*PAIR)), [wide(PAIR), wide(TWO)], "first"
    )(tile_mask, pair_state.reshape(PAIRS, CH), weight_in, gain_in)
    msg = exchange(msg, B)
    msg, lt0, rt0 = call(
        functools.partial(m_forward, 0), (shape(*ONE), shape(*FULL), shape(*FULL)),
        [wide(FULL)], "product0", smem=False,
    )(msg)
    msg = exchange(msg, 16)
    msg, inner0, middle, normed1 = call(
        k_second, (shape(*TWO), shape(*PAIR), shape(*PAIR), shape(*PAIR)),
        [wide(ONE), wide(PAIR), wide(TWO)], "second",
    )(tile_mask, msg, x, normed0, weight_in, weight_out, gain_in, gain_out)
    msg = exchange(msg, B)
    msg, lt1, rt1 = call(
        functools.partial(m_forward, 1), (shape(*ONE), shape(*FULL), shape(*FULL)),
        [wide(FULL)], "product1", smem=False,
    )(msg)
    msg = exchange(msg, 16)
    msg, updated, cot, dgate1 = call(
        k_third, (shape(*ONE), shape(*PAIR), shape(*PAIR), shape(*PAIR)),
        [wide(ONE), wide(PAIR), wide(PAIR), wide(PAIR), wide(ONE)], "third",
    )(tile_mask, msg, middle, normed1, cotangent.reshape(PAIRS, CH), weight_in, weight_out, gain_out)
    msg = exchange(msg, 16)
    (msg,) = call(
        functools.partial(m_backward, 1), (shape(*TWO),),
        [pltpu.VMEM(FULL, BF16), wide(FULL), wide(FULL)], "back1", smem=False,
    )(msg, lt1, rt1)
    msg = exchange(msg, B)
    msg, grad, dgate0 = call(
        k_fourth, (shape(*ONE), shape(*PAIR, dtype=F32), shape(*PAIR)),
        [wide(TWO), wide(PAIR), wide(ONE)], "fourth",
    )(tile_mask, msg, middle, normed1, cot, dgate1, inner0, normed0, weight_in, weight_out, gain_in, gain_out)
    msg = exchange(msg, 16)
    (msg,) = call(
        functools.partial(m_backward, 0), (shape(*TWO),),
        [pltpu.VMEM(FULL, BF16), wide(FULL), wide(FULL)], "back0", smem=False,
    )(msg, lt0, rt0)
    msg = exchange(msg, B)
    (pair_grad,) = call(
        k_fifth, (shape(*PAIR, dtype=F32),), [wide(TWO)], "fifth"
    )(tile_mask, msg, x, normed0, grad, dgate0, weight_in, gain_in)
    return updated.reshape(A, B, CH), pair_grad.reshape(A, B, CH)


def solution(mesh):
    return jax.shard_map(
        body,
        mesh=mesh,
        in_specs=(P("row", "col", None), P(), P(), P(), P(), P(), P("row", "col", None)),
        out_specs=(P("row", "col", None), P("row", "col", None)),
        check_vma=False,
    )
```

```python
import functools

import jax
import jax.numpy as jnp
from jax import lax
from jax.experimental import pallas as pl
from jax.experimental.pallas import tpu as pltpu
from jax.sharding import PartitionSpec as P

RES = 384
TILES = 3
TILE = RES // TILES
CH = 128
ROWS = 8
COLS = 16
A = RES // ROWS
B = RES // COLS
PAIRS = A * B
NB = 8
CHUNK = NB * A
F32 = jnp.float32
BF16 = jnp.bfloat16
EPS = 1e-05
AXES = ("row", "col")
VM = pl.BlockSpec(memory_space=pltpu.VMEM)
SM = pl.BlockSpec(memory_space=pltpu.SMEM)
HB = pl.BlockSpec(memory_space=pltpu.HBM)
DMA = pltpu.SemaphoreType.DMA
TWO_ROWS = 18
ONE_ROWS = 10


def mm(x, w):
    return lax.dot_general(x, w, (((1,), (0,)), ((), ())), preferred_element_type=F32)


def mm_nt(x, w):
    return lax.dot_general(x, w, (((1,), (1,)), ((), ())), preferred_element_type=F32)


def mm_tn(x, w):
    return lax.dot_general(x, w, (((0,), (0,)), ((), ())), preferred_element_type=F32)


def gate_chunk(mask_ref, b0):
    row_first = lax.axis_index("row") * A
    col_first = lax.axis_index("col") * B
    t0 = row_first // TILE
    t1 = jnp.minimum(t0 + 1, TILES - 1)
    low = lax.broadcasted_iota(jnp.int32, (A, CH), 0) < (t0 + 1) * TILE - row_first
    parts = []
    for k in range(NB):
        jt = (col_first + b0 + k) // TILE
        m0 = mask_ref[t0, jt].astype(F32)
        m1 = mask_ref[t1, jt].astype(F32)
        parts.append(jnp.where(low, jnp.full((A, CH), m0, F32), jnp.full((A, CH), m1, F32)))
    return jnp.concatenate(parts, axis=0)


def rows_of(chunk):
    return pl.ds(pl.multiple_of(chunk * CHUNK, CHUNK), CHUNK)


def load_turned(ref, b0):
    return jnp.concatenate([ref[pl.ds(b0 + k, A, stride=B), :] for k in range(NB)], axis=0)


def store_turned(ref, b0, value):
    for k in range(NB):
        ref[pl.ds(b0 + k, A, stride=B), :] = value[k * A:(k + 1) * A]


def pack_two(ref, i, left, right):
    parts = []
    for k in range(NB):
        parts += [left[k * A:(k + 1) * A], right[k * A:(k + 1) * A]]
    items = jnp.concatenate(parts, axis=0)
    for t in range(6):
        ref[pl.ds(i * 6 + t, CH, stride=TWO_ROWS), :] = jnp.transpose(items[t * 128:(t + 1) * 128])


def unpack_two(wide, i):
    items = jnp.concatenate(
        [jnp.transpose(wide[pl.ds(i * 6 + t, CH, stride=TWO_ROWS), :]) for t in range(6)], axis=0
    )
    lefts = [items[k * 2 * A:k * 2 * A + A] for k in range(NB)]
    rights = [items[k * 2 * A + A:(k + 1) * 2 * A] for k in range(NB)]
    return jnp.concatenate(lefts, axis=0), jnp.concatenate(rights, axis=0)


def pack_one(ref, i, value):
    for t in range(3):
        ref[pl.ds(i * 3 + t, CH, stride=ONE_ROWS), :] = jnp.transpose(value[t * 128:(t + 1) * 128])


def unpack_one(wide, i):
    return jnp.concatenate(
        [jnp.transpose(wide[pl.ds(i * 3 + t, CH, stride=ONE_ROWS), :]) for t in range(3)], axis=0
    )


def send_one(msg_ref, msgf):
    msgf[pl.ds(ONE_ROWS - 1, CH, stride=ONE_ROWS), :] = jnp.zeros((CH, CH), F32)
    msg_ref[...] = msgf[...].astype(BF16)


def chunks(fn):
    def step(i, carry):
        fn(i, i * NB)
        return carry

    lax.fori_loop(0, B // NB, step, 0)


def move(src, dst, sem):
    copy = pltpu.make_async_copy(src, dst, sem)
    copy.start()
    return copy


def average():
    return jnp.full((CH, CH), 1.0 / CH, BF16)


def normalize(values, short):
    center = values - mm(short, average())
    inv = lax.rsqrt(jnp.mean(center * center, axis=-1, keepdims=True) + EPS)
    return center * inv, inv


def centered(weight, gain_row):
    gain = jnp.transpose(jnp.broadcast_to(gain_row, (CH, CH)))
    scaled = weight.astype(F32) * jnp.concatenate([gain] * (weight.shape[1] // CH), axis=1)
    scaled = scaled - jnp.mean(scaled, axis=0, keepdims=True)
    high = scaled.astype(BF16)
    return high, (scaled - high.astype(F32)).astype(BF16)


def norm_back(standard, inv, scaled):
    return inv * (scaled - standard * jnp.mean(scaled * standard, axis=-1, keepdims=True))


def save_norm(refs, rows, standard, inv):
    refs[0][rows, :] = standard
    refs[1][rows, :] = jnp.broadcast_to(inv, standard.shape)


def open_gates(gate, proj, rows, gate_refs, fac_refs):
    sides = []
    for k in range(2):
        value = proj[:, 2 * k * CH:(2 * k + 1) * CH]
        sig = jax.nn.sigmoid(proj[:, (2 * k + 1) * CH:(2 * k + 2) * CH])
        factor = gate * sig
        side = factor * value
        fac_refs[2 * k][rows, :] = factor
        fac_refs[2 * k + 1][rows, :] = side * (1.0 - sig)
        sides.append(side)
    sig = jax.nn.sigmoid(proj[:, 4 * CH:])
    factor = gate * sig
    gate_refs[0][rows, :] = factor
    gate_refs[1][rows, :] = factor * (1.0 - sig)
    return sides


def k_first(far_mask_ref, pair_ref, win_ref, gin_ref, msg_ref, x_ref, *refs):
    norms, gates, facs = refs[:2], refs[2:4], refs[4:8]
    pair, win, gin, wide, msgf, mask_ref, sems = refs[8:]
    far = ((pair_ref, pair), (win_ref.at[0], win), (gin_ref, gin), (far_mask_ref, mask_ref))
    loads = [move(src, dst, sems.at[k]) for k, (src, dst) in enumerate(far)]
    loads[0].wait()
    wide[...] = pair[...].astype(F32)
    for copy in loads[1:]:
        copy.wait()

    def chunk(i, b0):
        rows = rows_of(i)
        x = load_turned(wide, b0)
        short = x.astype(BF16)
        x_ref[rows, :] = short
        standard, inv = normalize(x, short)
        save_norm(norms, rows, standard, inv)
        proj = mm((standard * gin[0:1, :]).astype(BF16), win[...])
        left, right = open_gates(gate_chunk(mask_ref, b0), proj, rows, gates, facs)
        pack_two(msgf, i, left, right)

    chunks(chunk)
    msg_ref[...] = msgf[...].astype(BF16)


def k_second(
    mask_ref, in_ref, x_ref, gsig_ref, slope_ref, win_ref, wout_ref, gin_ref, gout_ref,
    msg_ref, mid_ref, slope_out_ref, *refs
):
    norms0, norms1, gates, facs = refs[:2], refs[2:4], refs[4:6], refs[6:10]
    wide, msgf = refs[10:]
    wide[...] = in_ref[...].astype(F32)

    def chunk(i, b0):
        rows = rows_of(i)
        value = unpack_one(wide, i)
        standard, inv = normalize(value, value.astype(BF16))
        save_norm(norms0, rows, standard, inv)
        update = mm((standard * gout_ref[0:1, :]).astype(BF16), wout_ref[0])
        slope_out_ref[rows, :] = slope_ref[rows, :] * update
        middle = (x_ref[rows, :].astype(F32) + gsig_ref[rows, :] * update).astype(BF16)
        mid_ref[rows, :] = middle
        standard, inv = normalize(middle.astype(F32), middle)
        save_norm(norms1, rows, standard, inv)
        proj = mm((standard * gin_ref[1:2, :]).astype(BF16), win_ref[1])
        left, right = open_gates(gate_chunk(mask_ref, b0), proj, rows, gates, facs)
        pack_two(msgf, i, left, right)

    chunks(chunk)
    msg_ref[...] = msgf[...].astype(BF16)


def k_third(
    in_ref, mid_ref, gsig_ref, slope_ref, cot_ref, wout_ref, gout_ref,
    msg_ref, out_ref, cot_out_ref, dgate_ref, wide, cotf, outf, msgf, high, low,
):
    wide[...] = in_ref[...].astype(F32)
    cotf[...] = cot_ref[...].astype(F32)
    high[...], low[...] = centered(wout_ref[1], gout_ref[1:2, :])

    def chunk(i, b0):
        rows = rows_of(i)
        grad = load_turned(cotf, b0)
        cot_out_ref[rows, :] = grad.astype(BF16)
        gsig = gsig_ref[rows, :]
        d_update = (grad * gsig).astype(BF16)
        scaled = mm_nt(d_update, high[...]) + mm_nt(d_update, low[...])
        value = unpack_one(wide, i)
        standard, inv = normalize(value, value.astype(BF16))
        pack_one(msgf, i, norm_back(standard, inv, scaled))
        update = mm((standard * gout_ref[1:2, :]).astype(BF16), wout_ref[1])
        store_turned(outf, b0, mid_ref[rows, :].astype(F32) + gsig * update)
        dgate_ref[rows, :] = (grad * slope_ref[rows, :] * update).astype(BF16)

    chunks(chunk)
    out_ref[...] = outf[...].astype(BF16)
    send_one(msg_ref, msgf)


def bottom_back(d_left, d_right, dgate_ref, facs, norms, high, low, rows):
    d_proj = jnp.concatenate(
        [
            (d_left * facs[0][rows, :]).astype(BF16),
            (d_left * facs[1][rows, :]).astype(BF16),
            (d_right * facs[2][rows, :]).astype(BF16),
            (d_right * facs[3][rows, :]).astype(BF16),
            dgate_ref[rows, :],
        ],
        axis=1,
    )
    scaled = mm_nt(d_proj, high[...]) + mm_nt(d_proj, low[...])
    return norm_back(norms[0][rows, :], norms[1][rows, :], scaled)


def k_fourth(
    in_ref, cot_ref, dgate1_ref, f0, f1, f2, f3, n0, n1, gsig0_ref, slope0_ref, m0, m1,
    win_ref, wout_ref, gin_ref, gout_ref, msg_ref, grad_ref, dgate0_ref,
    wide, msgf, high, low, out_high, out_low,
):
    wide[...] = in_ref[...].astype(F32)
    high[...], low[...] = centered(win_ref[1], gin_ref[1:2, :])
    out_high[...], out_low[...] = centered(wout_ref[0], gout_ref[0:1, :])

    def chunk(i, b0):
        rows = rows_of(i)
        d_left, d_right = unpack_two(wide, i)
        grad = cot_ref[rows, :].astype(F32) + bottom_back(
            d_left, d_right, dgate1_ref, (f0, f1, f2, f3), (n0, n1), high, low, rows
        )
        grad_ref[rows, :] = grad
        dgate0_ref[rows, :] = (grad * slope0_ref[rows, :]).astype(BF16)
        d_update = (grad * gsig0_ref[rows, :]).astype(BF16)
        scaled = mm_nt(d_update, out_high[...]) + mm_nt(d_update, out_low[...])
        pack_one(msgf, i, norm_back(m0[rows, :], m1[rows, :], scaled))

    chunks(chunk)
    send_one(msg_ref, msgf)


def k_fifth(
    in_ref, grad_ref, dgate0_ref, f0, f1, f2, f3, n0, n1, win_ref, gin_ref, out_ref, wide, high, low
):
    wide[...] = in_ref[...].astype(F32)
    high[...], low[...] = centered(win_ref[0], gin_ref[0:1, :])

    def chunk(i, b0):
        rows = rows_of(i)
        d_left, d_right = unpack_two(wide, i)
        grad = grad_ref[rows, :] + bottom_back(
            d_left, d_right, dgate0_ref, (f0, f1, f2, f3), (n0, n1), high, low, rows
        )
        store_turned(out_ref, b0, grad)

    chunks(chunk)


def lanes(n):
    return lax.broadcasted_iota(jnp.int32, (n, 128), 1)


def turn(value, shift):
    shift = shift % 128
    return value if shift == 0 else pltpu.roll(value, shift, axis=1)


def thread(segments, lane):
    value = segments[-1][1]
    for (_, part), (end, _) in zip(reversed(segments[:-1]), reversed(segments[1:])):
        value = jnp.where(lane < end, part, value)
    return value


def inside(t):
    return [p for p in range(8) if p * A < (t + 1) * 128 and (p + 1) * A > t * 128]


def swap(load, n):
    lane = lanes(n)
    turned = []
    for d in range(8):
        tiles = []
        for t in range(3):
            parts = [(max(q * A - t * 128, 0), load((q + d) % 8, t)) for q in inside(t)]
            tiles.append(turn(thread(parts, lane), A * d))
        turned.append(tiles)
    for q in range(8):
        t0, off = divmod(q * A, 128)
        split = min(A, 128 - off)
        result = []
        for t in range(3):
            segments = []
            for p in inside(t):
                base = p * A - t * 128
                pieces = [(0, split, t0)] + ([(split, A, t0 + 1)] if split < A else [])
                for first, last, source in pieces:
                    if base + last > 0 and base + first < 128:
                        segments.append((max(base + first, 0), turned[(p - q) % 8][source]))
            result.append(thread(segments, lane))
        yield q, result


PART = 8


def narrow(tiles, dst):
    for t in range(3):
        dst[:, t * 128:(t + 1) * 128] = tiles[t * RES:(t + 1) * RES, :].astype(BF16)


def keep(tiles, value):
    for t in range(3):
        tiles[t * RES:(t + 1) * RES, :] = value[:, t * 128:(t + 1) * 128]


def join_two(x_ref, xf, lf, rf, lt, rt):
    xf[...] = x_ref[...].astype(F32)
    group = COLS * TWO_ROWS
    for n in range(0, 96, PART):
        def load(r, t):
            return xf[pl.ds(r * group + 3 * n + t, PART, stride=3), :]

        for p, tiles in swap(load, PART):
            dst = (lf, rf)[p % 2]
            for t in range(3):
                dst[pl.ds(t * RES + 4 * n + p // 2, PART, stride=4), :] = tiles[t]
    narrow(lf, lt)
    narrow(rf, rt)


def split_two(lf, rf, o_ref, of):
    group = COLS * TWO_ROWS
    for n in range(0, 96, PART):
        def load(p, t):
            return (lf, rf)[p % 2][pl.ds(t * RES + 4 * n + p // 2, PART, stride=4), :]

        for r, tiles in swap(load, PART):
            for t in range(3):
                of[pl.ds(r * group + 3 * n + t, PART, stride=3), :] = tiles[t]
    o_ref[...] = of[...].astype(BF16)


def join_one(x_ref, xf, df, dst):
    xf[...] = x_ref[...].astype(F32)
    group = COLS * ONE_ROWS
    for m in range(3):
        for c in range(0, COLS, PART):
            def load(r, t):
                return xf[pl.ds(r * group + c * ONE_ROWS + 3 * m + t, PART, stride=ONE_ROWS), :]

            for q, tiles in swap(load, PART):
                for t in range(3):
                    df[pl.ds(t * RES + c * B + 8 * m + q, PART, stride=B), :] = tiles[t]
    narrow(df, dst)


def split_one(value, o_ref, of):
    group = COLS * ONE_ROWS
    for m in range(3):
        for c in range(0, COLS, PART):
            def load(q, t):
                return value[pl.ds(t * RES + c * B + 8 * m + q, PART, stride=B), :]

            for r, tiles in swap(load, PART):
                for t in range(3):
                    of[pl.ds(r * group + c * ONE_ROWS + 3 * m + t, PART, stride=ONE_ROWS), :] = tiles[t]
    send_one(o_ref, of)


def m_forward(u, x_ref, o_ref, lt, rt, xf, lf, rf, prod, of):
    join_two(x_ref, xf, lf, rf, lt, rt)
    if u == 0:
        keep(prod, mm_tn(rt[...], lt[...]))
    else:
        keep(prod, mm_nt(rt[...], lt[...]))
    split_one(prod, o_ref, of)


def m_backward(u, x_ref, lt, rt, o_ref, xf, df, dt, prod_l, prod_r, of):
    join_one(x_ref, xf, df, dt)
    if u == 0:
        keep(prod_l, mm(rt[...], dt[...]))
        keep(prod_r, mm_nt(lt[...], dt[...]))
    else:
        keep(prod_l, mm_tn(dt[...], rt[...]))
        keep(prod_r, mm(dt[...], lt[...]))
    split_two(prod_l, prod_r, o_ref, of)


def shape(*dims, dtype=BF16):
    return jax.ShapeDtypeStruct(dims, dtype)


def call(fn, outs, scratch, name, smem=False, far=()):
    def run(*args):
        specs = [HB if k in far else VM for k in range(len(args))]
        args = [
            pltpu.with_memory_space_constraint(a, pltpu.HBM) if k in far else a
            for k, a in enumerate(args)
        ]
        if smem:
            specs[0] = SM
        return pl.pallas_call(
            fn,
            out_shape=outs,
            in_specs=specs,
            out_specs=[VM] * len(outs),
            scratch_shapes=scratch,
            compiler_params=pltpu.CompilerParams(vmem_limit_bytes=16 * 1024 * 1024),
            name=name,
        )(*args)

    return run


def exchange(message, rows):
    message = message.reshape(ROWS * COLS, rows // 2, 2, 128)
    return lax.all_to_all(message, AXES, 0, 0, tiled=True).reshape(ROWS * COLS * rows, 128)


TWO = (CH * TWO_ROWS, 128)
ONE = (CH * ONE_ROWS, 128)
PAIR = (PAIRS, CH)
FULL = (RES, RES)
TILED = (3 * RES, 128)
KEEP = shape(*PAIR)
WIDE = shape(*PAIR, dtype=F32)


def wide(dims):
    return pltpu.VMEM(dims, F32)


def body(pair_state, tile_mask, weight_in, weight_out, gain_in, gain_out, cotangent):
    w, wo, gi, go = weight_in, weight_out, gain_in, gain_out
    full = shape(*FULL)
    square = pltpu.VMEM((CH, CH), BF16)
    broad = pltpu.VMEM((CH, 5 * CH), BF16)
    forward = [wide(TWO), wide(TILED), wide(TILED), wide(TILED), wide(ONE)]
    backward = [wide(ONE), wide(TILED), pltpu.VMEM(FULL, BF16), wide(TILED), wide(TILED), wide(TWO)]
    msg, x, n0, n1, gsig0, slope0, *fac0 = call(
        k_first, (shape(*TWO), KEEP) + (WIDE,) * 8,
        [pltpu.VMEM(PAIR, BF16), broad, wide((2, CH)), wide(PAIR), wide(TWO),
         pltpu.SMEM((TILES, TILES), jnp.int32), DMA((4,))],
        "first", far=(0, 1, 2, 3),
    )(tile_mask, pair_state.reshape(PAIRS, CH), w, gi)
    norm_x = (n0, n1)
    msg = exchange(msg, TWO_ROWS)
    msg, lt0, rt0 = call(
        functools.partial(m_forward, 0), (shape(*ONE), full, full), forward, "product0"
    )(msg)
    msg = exchange(msg, ONE_ROWS)
    msg, middle, slope0, i0, i1, m0, m1, gsig1, slope1, *fac1 = call(
        k_second, (shape(*TWO), KEEP) + (WIDE,) * 11, [wide(ONE), wide(TWO)], "second", smem=True
    )(tile_mask, msg, x, gsig0, slope0, w, wo, gi, go)
    msg = exchange(msg, TWO_ROWS)
    msg, lt1, rt1 = call(
        functools.partial(m_forward, 1), (shape(*ONE), full, full), forward, "product1"
    )(msg)
    msg = exchange(msg, ONE_ROWS)
    msg, updated, cot, dgate1 = call(
        k_third, (shape(*ONE), KEEP, KEEP, KEEP),
        [wide(ONE), wide(PAIR), wide(PAIR), wide(ONE), square, square], "third",
    )(msg, middle, gsig1, slope1, cotangent.reshape(PAIRS, CH), wo, go)
    msg = exchange(msg, ONE_ROWS)
    (msg,) = call(functools.partial(m_backward, 1), (shape(*TWO),), backward, "back1")(msg, lt1, rt1)
    msg = exchange(msg, TWO_ROWS)
    msg, grad, dgate0 = call(
        k_fourth, (shape(*ONE), WIDE, KEEP),
        [wide(TWO), wide(ONE), broad, broad, square, square], "fourth",
    )(msg, cot, dgate1, *fac1, m0, m1, gsig0, slope0, i0, i1, w, wo, gi, go)
    msg = exchange(msg, ONE_ROWS)
    (msg,) = call(functools.partial(m_backward, 0), (shape(*TWO),), backward, "back0")(msg, lt0, rt0)
    msg = exchange(msg, TWO_ROWS)
    (pair_grad,) = call(k_fifth, (WIDE,), [wide(TWO), broad, broad], "fifth")(
        msg, grad, dgate0, *fac0, *norm_x, w, gi
    )
    return updated.reshape(A, B, CH), pair_grad.reshape(A, B, CH)


def solution(mesh):
    return jax.shard_map(
        body,
        mesh=mesh,
        in_specs=(P("row", "col", None), P(), P(), P(), P(), P(), P("row", "col", None)),
        out_specs=(P("row", "col", None), P("row", "col", None)),
        check_vma=False,
    )
```

```python
import functools

import jax
import jax.numpy as jnp
from jax import lax
from jax.experimental import pallas as pl
from jax.experimental.pallas import tpu as pltpu
from jax.sharding import PartitionSpec as P

RES = 384
TILES = 3
TILE = RES // TILES
CH = 128
ROWS = 8
COLS = 16
A = RES // ROWS
B = RES // COLS
PAIRS = A * B
NB = 24
CHUNK = NB * A
F32 = jnp.float32
BF16 = jnp.bfloat16
EPS = 1e-05
AXES = ("row", "col")
VM = pl.BlockSpec(memory_space=pltpu.VMEM)
HB = pl.BlockSpec(memory_space=pltpu.HBM)
DMA = pltpu.SemaphoreType.DMA
TWO_ROWS = 18
ONE_ROWS = 10


def mm(x, w):
    return lax.dot_general(x, w, (((1,), (0,)), ((), ())), preferred_element_type=F32)


def mm_nt(x, w):
    return lax.dot_general(x, w, (((1,), (1,)), ((), ())), preferred_element_type=F32)


def mm_tn(x, w):
    return lax.dot_general(x, w, (((0,), (0,)), ((), ())), preferred_element_type=F32)


def gate_chunk(mask_ref, b0):
    row_first = lax.axis_index("row") * A
    col_first = lax.axis_index("col") * B
    t0 = row_first // TILE
    t1 = jnp.minimum(t0 + 1, TILES - 1)
    low = lax.broadcasted_iota(jnp.int32, (A, CH), 0) < (t0 + 1) * TILE - row_first
    parts = []
    for k in range(NB):
        jt = (col_first + b0 + k) // TILE
        m0 = mask_ref[t0, jt].astype(F32)
        m1 = mask_ref[t1, jt].astype(F32)
        parts.append(jnp.where(low, jnp.full((A, CH), m0, F32), jnp.full((A, CH), m1, F32)))
    return jnp.concatenate(parts, axis=0)


def rows_of(chunk, nb=NB):
    return pl.ds(chunk * nb * A, nb * A)


def load_turned(ref, b0):
    return jnp.concatenate([ref[pl.ds(b0 + k, A, stride=B), :] for k in range(NB)], axis=0)


def store_turned(ref, b0, value):
    for k in range(NB):
        ref[pl.ds(b0 + k, A, stride=B), :] = value[k * A:(k + 1) * A]


def pack_two(ref, i, left, right):
    parts = []
    for k in range(NB):
        parts += [left[k * A:(k + 1) * A], right[k * A:(k + 1) * A]]
    items = jnp.concatenate(parts, axis=0)
    for t in range(NB * 2 * A // 128):
        ref[pl.ds(i * (NB * 2 * A // 128) + t, CH, stride=TWO_ROWS), :] = jnp.transpose(items[t * 128:(t + 1) * 128])


def unpack_two(wide, i, nb=NB):
    blocks = nb * 2 * A // 128
    items = jnp.concatenate(
        [jnp.transpose(wide[pl.ds(i * blocks + t, CH, stride=TWO_ROWS), :]) for t in range(blocks)],
        axis=0,
    )
    lefts = [items[k * 2 * A:k * 2 * A + A] for k in range(nb)]
    rights = [items[k * 2 * A + A:(k + 1) * 2 * A] for k in range(nb)]
    return jnp.concatenate(lefts, axis=0), jnp.concatenate(rights, axis=0)


def pack_one(ref, i, value):
    for t in range(NB * A // 128):
        ref[pl.ds(i * (NB * A // 128) + t, CH, stride=ONE_ROWS), :] = jnp.transpose(value[t * 128:(t + 1) * 128])


def unpack_one(wide, i):
    return jnp.concatenate(
        [jnp.transpose(wide[pl.ds(i * (NB * A // 128) + t, CH, stride=ONE_ROWS), :])
         for t in range(NB * A // 128)], axis=0
    )


def send_one(msg_ref, msgf):
    msgf[pl.ds(ONE_ROWS - 1, CH, stride=ONE_ROWS), :] = jnp.zeros((CH, CH), F32)
    msg_ref[...] = msgf[...].astype(BF16)


def chunks(fn):
    for i in range(B // NB):
        fn(i, i * NB)


def move(src, dst, sem):
    copy = pltpu.make_async_copy(src, dst, sem)
    copy.start()
    return copy


def average():
    return jnp.full((CH, CH), 1.0 / CH, BF16)


def normalize(values, short):
    center = values - mm(short, average())
    inv = lax.rsqrt(jnp.mean(center * center, axis=-1, keepdims=True) + EPS)
    return center * inv, inv


def centered(weight, gain_row):
    gain = jnp.transpose(jnp.broadcast_to(gain_row, (CH, CH)))
    scaled = weight.astype(F32) * jnp.concatenate([gain] * (weight.shape[1] // CH), axis=1)
    scaled = scaled - jnp.mean(scaled, axis=0, keepdims=True)
    high = scaled.astype(BF16)
    return jnp.concatenate([high, (scaled - high.astype(F32)).astype(BF16)], axis=0)


def mm_centered(value, weight):
    both = mm_nt(value, weight)
    return both[:, :CH] + both[:, CH:]


def norm_back(standard, inv, scaled):
    return inv * (scaled - standard * jnp.mean(scaled * standard, axis=-1, keepdims=True))


def save_norm(refs, rows, standard, inv):
    refs[0][rows, :] = standard
    refs[1][rows, :] = jnp.broadcast_to(inv, standard.shape)


def open_gates(gate, proj, rows, gate_refs, fac_refs):
    sides = []
    for k in range(2):
        value = proj[:, 2 * k * CH:(2 * k + 1) * CH]
        sig = jax.nn.sigmoid(proj[:, (2 * k + 1) * CH:(2 * k + 2) * CH])
        factor = gate * sig
        side = factor * value
        fac_refs[2 * k][rows, :] = factor
        fac_refs[2 * k + 1][rows, :] = side * (1.0 - sig)
        sides.append(side)
    sig = jax.nn.sigmoid(proj[:, 4 * CH:])
    factor = gate * sig
    gate_refs[0][rows, :] = factor
    gate_refs[1][rows, :] = factor * (1.0 - sig)
    return sides


def k_first(far_mask_ref, pair_ref, win_ref, gin_ref, msg_ref, x_ref, gate_ref, gain_ref, *refs):
    norms, gates, facs = refs[:2], refs[2:4], refs[4:8]
    pair, win, gin, wide, msgf, mask_ref, sems = refs[8:]
    far = ((pair_ref, pair), (win_ref.at[0], win), (gin_ref, gin), (far_mask_ref, mask_ref))
    loads = [move(src, dst, sems.at[k]) for k, (src, dst) in enumerate(far)]
    loads[0].wait()
    wide[...] = pair[...].astype(F32)
    for copy in loads[1:]:
        copy.wait()
    gain_ref[...] = gin[...]

    def chunk(i, b0):
        rows = rows_of(i)
        x = load_turned(wide, b0)
        short = x.astype(BF16)
        x_ref[rows, :] = short
        standard, inv = normalize(x, short)
        save_norm(norms, rows, standard, inv)
        proj = mm((standard * gin[0:1, :]).astype(BF16), win[...])
        gate = gate_chunk(mask_ref, b0)
        gate_ref[rows, :] = gate
        left, right = open_gates(gate, proj, rows, gates, facs)
        pack_two(msgf, i, left, right)

    chunks(chunk)
    msg_ref[...] = msgf[...].astype(BF16)


def k_second(
    gate_ref, in_ref, x_ref, gsig_ref, slope_ref, win_ref, wout_ref, gin_ref, gout_ref,
    msg_ref, mid_ref, slope_out_ref, *refs
):
    norms0, norms1, gates, facs = refs[:2], refs[2:4], refs[4:6], refs[6:10]
    wide, msgf = refs[10:]
    wide[...] = in_ref[...].astype(F32)

    def chunk(i, b0):
        rows = rows_of(i)
        value = unpack_one(wide, i)
        standard, inv = normalize(value, value.astype(BF16))
        save_norm(norms0, rows, standard, inv)
        update = mm((standard * gout_ref[0:1, :]).astype(BF16), wout_ref[0])
        slope_out_ref[rows, :] = slope_ref[rows, :] * update
        middle = (x_ref[rows, :].astype(F32) + gsig_ref[rows, :] * update).astype(BF16)
        mid_ref[rows, :] = middle
        standard, inv = normalize(middle.astype(F32), middle)
        save_norm(norms1, rows, standard, inv)
        proj = mm((standard * gin_ref[1:2, :]).astype(BF16), win_ref[1])
        left, right = open_gates(gate_ref[rows, :], proj, rows, gates, facs)
        pack_two(msgf, i, left, right)

    chunks(chunk)
    msg_ref[...] = msgf[...].astype(BF16)


def k_third(
    in_ref, mid_ref, gsig_ref, slope_ref, cot_ref, wout_ref, gout_ref,
    msg_ref, out_ref, cot_out_ref, dgate_ref, wide, cotf, outf, msgf, back, out, sems,
):
    wide[...] = in_ref[...].astype(F32)
    cotf[...] = cot_ref[...].astype(F32)
    back[...] = centered(wout_ref[1], gout_ref[1:2, :])

    def chunk(i, b0):
        rows = rows_of(i)
        grad = load_turned(cotf, b0)
        cot_out_ref[rows, :] = grad.astype(BF16)
        gsig = gsig_ref[rows, :]
        d_update = (grad * gsig).astype(BF16)
        scaled = mm_centered(d_update, back[...])
        value = unpack_one(wide, i)
        standard, inv = normalize(value, value.astype(BF16))
        update = mm((standard * gout_ref[1:2, :]).astype(BF16), wout_ref[1])
        store_turned(outf, b0, mid_ref[rows, :].astype(F32) + gsig * update)
        out[...] = outf[...].astype(BF16)
        saves.append(move(out, out_ref, sems.at[0]))
        dgate_ref[rows, :] = (grad * slope_ref[rows, :] * update).astype(BF16)
        pack_one(msgf, i, norm_back(standard, inv, scaled))

    saves = []
    chunks(chunk)
    send_one(msg_ref, msgf)
    saves[0].wait()


def bottom_back(d_left, d_right, dgate_ref, facs, norms, back, rows):
    d_proj = jnp.concatenate(
        [
            (d_left * facs[0][rows, :]).astype(BF16),
            (d_left * facs[1][rows, :]).astype(BF16),
            (d_right * facs[2][rows, :]).astype(BF16),
            (d_right * facs[3][rows, :]).astype(BF16),
            dgate_ref[rows, :],
        ],
        axis=1,
    )
    return norm_back(norms[0][rows, :], norms[1][rows, :], mm_centered(d_proj, back[...]))


def k_fourth(
    in_ref, cot_ref, dgate1_ref, f0, f1, f2, f3, n0, n1, gsig0_ref, slope0_ref, m0, m1,
    win_ref, wout_ref, gin_ref, gout_ref, msg_ref, grad_ref, dgate0_ref,
    wide, msgf, back, out_back,
):
    wide[...] = in_ref[...].astype(F32)
    back[...] = centered(win_ref[1], gin_ref[1:2, :])
    out_back[...] = centered(wout_ref[0], gout_ref[0:1, :])

    def chunk(i, b0):
        rows = rows_of(i)
        d_left, d_right = unpack_two(wide, i)
        grad = cot_ref[rows, :].astype(F32) + bottom_back(
            d_left, d_right, dgate1_ref, (f0, f1, f2, f3), (n0, n1), back, rows
        )
        grad_ref[rows, :] = grad
        dgate0_ref[rows, :] = (grad * slope0_ref[rows, :]).astype(BF16)
        d_update = (grad * gsig0_ref[rows, :]).astype(BF16)
        scaled = mm_centered(d_update, out_back[...])
        pack_one(msgf, i, norm_back(m0[rows, :], m1[rows, :], scaled))

    chunks(chunk)
    send_one(msg_ref, msgf)


PIECE = 8


def k_fifth(
    in_ref, grad_ref, dgate0_ref, f0, f1, f2, f3, n0, n1, win_ref, gin_ref, out_ref,
    wide, back, outf, sems,
):
    wide[...] = in_ref[...].astype(F32)
    back[...] = centered(win_ref[0], gin_ref[0:1, :])
    saves = []
    for i in range(B // PIECE):
        rows = rows_of(i, PIECE)
        d_left, d_right = unpack_two(wide, i, PIECE)
        grad = grad_ref[rows, :] + bottom_back(
            d_left, d_right, dgate0_ref, (f0, f1, f2, f3), (n0, n1), back, rows
        )
        for k in range(PIECE):
            outf[pl.ds(i * PIECE + k, A, stride=B), :] = grad[k * A:(k + 1) * A]
        part = pl.ds(i * PIECE, PIECE)
        saves.append(move(outf.reshape(A, B, CH).at[:, part, :], out_ref.at[:, part, :], sems.at[i]))
    for copy in saves:
        copy.wait()


def lanes(n):
    return lax.broadcasted_iota(jnp.int32, (n, 128), 1)


def turn(value, shift):
    shift = shift % 128
    return value if shift == 0 else pltpu.roll(value, shift, axis=1)


def thread(segments, lane):
    value = segments[-1][1]
    for (_, part), (end, _) in zip(reversed(segments[:-1]), reversed(segments[1:])):
        value = jnp.where(lane < end, part, value)
    return value


def inside(t):
    return [p for p in range(8) if p * A < (t + 1) * 128 and (p + 1) * A > t * 128]


def swap(load, n):
    lane = lanes(n)
    turned = []
    for d in range(8):
        tiles = []
        for t in range(3):
            parts = [(max(q * A - t * 128, 0), load((q + d) % 8, t)) for q in inside(t)]
            tiles.append(turn(thread(parts, lane), A * d))
        turned.append(tiles)
    for q in range(8):
        t0, off = divmod(q * A, 128)
        split = min(A, 128 - off)
        result = []
        for t in range(3):
            segments = []
            for p in inside(t):
                base = p * A - t * 128
                pieces = [(0, split, t0)] + ([(split, A, t0 + 1)] if split < A else [])
                for first, last, source in pieces:
                    if base + last > 0 and base + first < 128:
                        segments.append((max(base + first, 0), turned[(p - q) % 8][source]))
            result.append(thread(segments, lane))
        yield q, result


PART = 8


def narrow(tiles, dst):
    for t in range(3):
        dst[:, t * 128:(t + 1) * 128] = tiles[t * RES:(t + 1) * RES, :].astype(BF16)


def keep(tiles, value):
    for t in range(3):
        tiles[t * RES:(t + 1) * RES, :] = value[:, t * 128:(t + 1) * 128]


def join_two(x_ref, xf, lf, rf, lt, rt):
    xf[...] = x_ref[...].astype(F32)
    group = COLS * TWO_ROWS
    for n in range(0, 96, PART):
        def load(r, t):
            return xf[pl.ds(r * group + 3 * n + t, PART, stride=3), :]

        for p, tiles in swap(load, PART):
            dst = (lf, rf)[p % 2]
            for t in range(3):
                dst[pl.ds(t * RES + 4 * n + p // 2, PART, stride=4), :] = tiles[t]
    narrow(lf, lt)
    narrow(rf, rt)


def split_two(lf, rf, o_ref, of):
    group = COLS * TWO_ROWS
    for n in range(0, 96, PART):
        def load(p, t):
            return (lf, rf)[p % 2][pl.ds(t * RES + 4 * n + p // 2, PART, stride=4), :]

        for r, tiles in swap(load, PART):
            for t in range(3):
                of[pl.ds(r * group + 3 * n + t, PART, stride=3), :] = tiles[t]
    o_ref[...] = of[...].astype(BF16)


def join_one(x_ref, xf, df, dst):
    xf[...] = x_ref[...].astype(F32)
    group = COLS * ONE_ROWS
    for m in range(3):
        for c in range(0, COLS, PART):
            def load(r, t):
                return xf[pl.ds(r * group + c * ONE_ROWS + 3 * m + t, PART, stride=ONE_ROWS), :]

            for q, tiles in swap(load, PART):
                for t in range(3):
                    df[pl.ds(t * RES + c * B + 8 * m + q, PART, stride=B), :] = tiles[t]
    narrow(df, dst)


def split_one(value, o_ref, of):
    group = COLS * ONE_ROWS
    for m in range(3):
        for c in range(0, COLS, PART):
            def load(q, t):
                return value[pl.ds(t * RES + c * B + 8 * m + q, PART, stride=B), :]

            for r, tiles in swap(load, PART):
                for t in range(3):
                    of[pl.ds(r * group + c * ONE_ROWS + 3 * m + t, PART, stride=ONE_ROWS), :] = tiles[t]
    send_one(o_ref, of)


def m_forward(u, x_ref, o_ref, lt, rt, xf, lf, rf, prod, of):
    join_two(x_ref, xf, lf, rf, lt, rt)
    if u == 0:
        keep(prod, mm_tn(rt[...], lt[...]))
    else:
        keep(prod, mm_nt(rt[...], lt[...]))
    split_one(prod, o_ref, of)


def m_backward(u, x_ref, lt, rt, o_ref, xf, df, dt, prod_l, prod_r, of):
    join_one(x_ref, xf, df, dt)
    if u == 0:
        keep(prod_l, mm(rt[...], dt[...]))
        keep(prod_r, mm_nt(lt[...], dt[...]))
    else:
        keep(prod_l, mm_tn(dt[...], rt[...]))
        keep(prod_r, mm(dt[...], lt[...]))
    split_two(prod_l, prod_r, o_ref, of)


def shape(*dims, dtype=BF16):
    return jax.ShapeDtypeStruct(dims, dtype)


def call(fn, outs, scratch, name, far=(), far_out=()):
    def run(*args):
        specs = [HB if k in far else VM for k in range(len(args))]
        args = [
            pltpu.with_memory_space_constraint(a, pltpu.HBM) if k in far else a
            for k, a in enumerate(args)
        ]
        return pl.pallas_call(
            fn,
            out_shape=outs,
            in_specs=specs,
            out_specs=[HB if k in far_out else VM for k in range(len(outs))],
            scratch_shapes=scratch,
            compiler_params=pltpu.CompilerParams(vmem_limit_bytes=16 * 1024 * 1024),
            name=name,
        )(*args)

    return run


def exchange(message, rows):
    message = message.reshape(ROWS * COLS, rows // 2, 2, 128)
    return lax.all_to_all(message, AXES, 0, 0, tiled=True).reshape(ROWS * COLS * rows, 128)


TWO = (CH * TWO_ROWS, 128)
ONE = (CH * ONE_ROWS, 128)
PAIR = (PAIRS, CH)
FULL = (RES, RES)
TILED = (3 * RES, 128)
KEEP = shape(*PAIR)
WIDE = shape(*PAIR, dtype=F32)


def wide(dims):
    return pltpu.VMEM(dims, F32)


def body(pair_state, tile_mask, weight_in, weight_out, gain_in, gain_out, cotangent):
    w, wo, gi, go = weight_in, weight_out, gain_in, gain_out
    full = shape(*FULL)
    square = pltpu.VMEM((2 * CH, CH), BF16)
    broad = pltpu.VMEM((2 * CH, 5 * CH), BF16)
    forward = [wide(TWO), wide(TILED), wide(TILED), wide(TILED), wide(ONE)]
    backward = [wide(ONE), wide(TILED), pltpu.VMEM(FULL, BF16), wide(TILED), wide(TILED), wide(TWO)]
    msg, x, gate, gi, n0, n1, gsig0, slope0, *fac0 = call(
        k_first, (shape(*TWO), KEEP, WIDE, shape(2, CH, dtype=F32)) + (WIDE,) * 8,
        [pltpu.VMEM(PAIR, BF16), pltpu.VMEM((CH, 5 * CH), BF16), wide((2, CH)), wide(PAIR), wide(TWO),
         pltpu.SMEM((TILES, TILES), jnp.int32), DMA((4,))],
        "first", far=(0, 1, 2, 3),
    )(tile_mask, pair_state.reshape(PAIRS, CH), w, gi)
    norm_x = (n0, n1)
    msg = exchange(msg, TWO_ROWS)
    msg, lt0, rt0 = call(
        functools.partial(m_forward, 0), (shape(*ONE), full, full), forward, "product0"
    )(msg)
    msg = exchange(msg, ONE_ROWS)
    msg, middle, slope0, i0, i1, m0, m1, gsig1, slope1, *fac1 = call(
        k_second, (shape(*TWO), KEEP) + (WIDE,) * 11, [wide(ONE), wide(TWO)], "second"
    )(gate, msg, x, gsig0, slope0, w, wo, gi, go)
    msg = exchange(msg, TWO_ROWS)
    msg, lt1, rt1 = call(
        functools.partial(m_forward, 1), (shape(*ONE), full, full), forward, "product1"
    )(msg)
    msg = exchange(msg, ONE_ROWS)
    msg, updated, cot, dgate1 = call(
        k_third, (shape(*ONE), pltpu.HBM(PAIR, BF16), KEEP, KEEP),
        [wide(ONE), wide(PAIR), wide(PAIR), wide(ONE), square,
         pltpu.VMEM(PAIR, BF16), DMA((1,))], "third", far_out=(1,),
    )(msg, middle, gsig1, slope1, cotangent.reshape(PAIRS, CH), wo, go)
    msg = exchange(msg, ONE_ROWS)
    (msg,) = call(functools.partial(m_backward, 1), (shape(*TWO),), backward, "back1")(msg, lt1, rt1)
    msg = exchange(msg, TWO_ROWS)
    msg, grad, dgate0 = call(
        k_fourth, (shape(*ONE), WIDE, KEEP),
        [wide(TWO), wide(ONE), broad, square], "fourth",
    )(msg, cot, dgate1, *fac1, m0, m1, gsig0, slope0, i0, i1, w, wo, gi, go)
    msg = exchange(msg, ONE_ROWS)
    (msg,) = call(functools.partial(m_backward, 0), (shape(*TWO),), backward, "back0")(msg, lt0, rt0)
    msg = exchange(msg, TWO_ROWS)
    (pair_grad,) = call(
        k_fifth, (pltpu.HBM((A, B, CH), F32),),
        [wide(TWO), broad, wide(PAIR), DMA((B // PIECE,))], "fifth", far_out=(0,),
    )(msg, grad, dgate0, *fac0, *norm_x, w, gi)
    return updated.reshape(A, B, CH), pair_grad


def solution(mesh):
    return jax.shard_map(
        body,
        mesh=mesh,
        in_specs=(P("row", "col", None), P(), P(), P(), P(), P(), P("row", "col", None)),
        out_specs=(P("row", "col", None), P("row", "col", None)),
        check_vma=False,
    )
```

```python
import functools

import jax
import jax.numpy as jnp
from jax import lax
from jax.experimental import pallas as pl
from jax.experimental.pallas import tpu as pltpu
from jax.sharding import PartitionSpec as P

RES = 384
TILES = 3
TILE = RES // TILES
CH = 128
ROWS = 8
COLS = 16
A = RES // ROWS
B = RES // COLS
PAIRS = A * B
NB = 24
CHUNK = NB * A
F32 = jnp.float32
BF16 = jnp.bfloat16
EPS = 1e-05
AXES = ("row", "col")
VM = pl.BlockSpec(memory_space=pltpu.VMEM)
HB = pl.BlockSpec(memory_space=pltpu.HBM)
DMA = pltpu.SemaphoreType.DMA
TWO_ROWS = 18
ONE_ROWS = 10


def mm(x, w):
    return lax.dot_general(x, w, (((1,), (0,)), ((), ())), preferred_element_type=F32)


def mm_nt(x, w):
    return lax.dot_general(x, w, (((1,), (1,)), ((), ())), preferred_element_type=F32)


def mm_tn(x, w):
    return lax.dot_general(x, w, (((0,), (0,)), ((), ())), preferred_element_type=F32)


def gate_chunk(mask_ref, b0):
    row_first = lax.axis_index("row") * A
    col_first = lax.axis_index("col") * B
    t0 = row_first // TILE
    t1 = jnp.minimum(t0 + 1, TILES - 1)
    low = lax.broadcasted_iota(jnp.int32, (A, CH), 0) < (t0 + 1) * TILE - row_first
    parts = []
    for k in range(NB):
        jt = (col_first + b0 + k) // TILE
        m0 = mask_ref[t0, jt].astype(F32)
        m1 = mask_ref[t1, jt].astype(F32)
        parts.append(jnp.where(low, jnp.full((A, CH), m0, F32), jnp.full((A, CH), m1, F32)))
    return jnp.concatenate(parts, axis=0)


def rows_of(chunk, nb=NB):
    return pl.ds(chunk * nb * A, nb * A)


def load_turned(ref, b0):
    return jnp.concatenate([ref[pl.ds(b0 + k, A, stride=B), :] for k in range(NB)], axis=0)


def store_turned(ref, b0, value):
    for k in range(NB):
        ref[pl.ds(b0 + k, A, stride=B), :] = value[k * A:(k + 1) * A]


def pack_two(ref, i, left, right):
    parts = []
    for k in range(NB):
        parts += [left[k * A:(k + 1) * A], right[k * A:(k + 1) * A]]
    items = jnp.concatenate(parts, axis=0)
    for t in range(NB * 2 * A // 128):
        ref[pl.ds(i * (NB * 2 * A // 128) + t, CH, stride=TWO_ROWS), :] = jnp.transpose(items[t * 128:(t + 1) * 128])


def unpack_two(wide, i, nb=NB):
    blocks = nb * 2 * A // 128
    items = jnp.concatenate(
        [jnp.transpose(wide[pl.ds(i * blocks + t, CH, stride=TWO_ROWS), :]) for t in range(blocks)],
        axis=0,
    )
    lefts = [items[k * 2 * A:k * 2 * A + A] for k in range(nb)]
    rights = [items[k * 2 * A + A:(k + 1) * 2 * A] for k in range(nb)]
    return jnp.concatenate(lefts, axis=0), jnp.concatenate(rights, axis=0)


def pack_one(ref, i, value):
    for t in range(NB * A // 128):
        ref[pl.ds(i * (NB * A // 128) + t, CH, stride=ONE_ROWS), :] = jnp.transpose(value[t * 128:(t + 1) * 128])


def unpack_one(wide, i):
    return jnp.concatenate(
        [jnp.transpose(wide[pl.ds(i * (NB * A // 128) + t, CH, stride=ONE_ROWS), :])
         for t in range(NB * A // 128)], axis=0
    )


def send_one(msg_ref, msgf):
    msgf[pl.ds(ONE_ROWS - 1, CH, stride=ONE_ROWS), :] = jnp.zeros((CH, CH), F32)
    msg_ref[...] = msgf[...].astype(BF16)


def chunks(fn):
    for i in range(B // NB):
        fn(i, i * NB)


def move(src, dst, sem):
    copy = pltpu.make_async_copy(src, dst, sem)
    copy.start()
    return copy


def average():
    return jnp.full((CH, CH), 1.0 / CH, BF16)


def normalize(values, short):
    center = values - mm(short, average())
    inv = lax.rsqrt(jnp.mean(center * center, axis=-1, keepdims=True) + EPS)
    return center * inv, inv


def centered(weight, gain_row):
    gain = jnp.transpose(jnp.broadcast_to(gain_row, (CH, CH)))
    scaled = weight.astype(F32) * jnp.concatenate([gain] * (weight.shape[1] // CH), axis=1)
    scaled = scaled - jnp.mean(scaled, axis=0, keepdims=True)
    high = scaled.astype(BF16)
    return jnp.concatenate([high, (scaled - high.astype(F32)).astype(BF16)], axis=0)


def mm_centered(value, weight):
    both = mm_nt(value, weight)
    return both[:, :CH] + both[:, CH:]


def norm_back(standard, inv, scaled):
    return inv * (scaled - standard * jnp.mean(scaled * standard, axis=-1, keepdims=True))


def save_norm(refs, rows, standard, inv):
    refs[0][rows, :] = standard
    refs[1][rows, :] = jnp.broadcast_to(inv, standard.shape)


def open_gates(gate, proj, rows, gate_refs, fac_refs):
    sides = []
    for k in range(2):
        value = proj[:, 2 * k * CH:(2 * k + 1) * CH]
        sig = jax.nn.sigmoid(proj[:, (2 * k + 1) * CH:(2 * k + 2) * CH])
        factor = gate * sig
        side = factor * value
        fac_refs[2 * k][rows, :] = factor
        fac_refs[2 * k + 1][rows, :] = side * (1.0 - sig)
        sides.append(side)
    sig = jax.nn.sigmoid(proj[:, 4 * CH:])
    factor = gate * sig
    gate_refs[0][rows, :] = factor
    gate_refs[1][rows, :] = factor * (1.0 - sig)
    return sides


def k_first(
    far_mask_ref, pair_ref, win_ref, gin_ref, gout_ref, msg_ref, x_ref, gate_ref, gain_ref, gain_out_ref, *refs
):
    norms, gates, facs = refs[:2], refs[2:4], refs[4:8]
    pair, win, gin, gout, wide, msgf, mask_ref, sems = refs[8:]
    far = ((pair_ref, pair), (win_ref.at[0], win), (gin_ref, gin), (gout_ref, gout), (far_mask_ref, mask_ref))
    loads = [move(src, dst, sems.at[k]) for k, (src, dst) in enumerate(far)]
    loads[0].wait()
    wide[...] = pair[...].astype(F32)
    for copy in loads[1:]:
        copy.wait()
    gain_out_ref[...] = gout[...]
    gain_ref[...] = gin[...]

    def chunk(i, b0):
        rows = rows_of(i)
        x = load_turned(wide, b0)
        short = x.astype(BF16)
        x_ref[rows, :] = short
        standard, inv = normalize(x, short)
        save_norm(norms, rows, standard, inv)
        proj = mm((standard * gin[0:1, :]).astype(BF16), win[...])
        gate = gate_chunk(mask_ref, b0)
        gate_ref[rows, :] = gate
        left, right = open_gates(gate, proj, rows, gates, facs)
        pack_two(msgf, i, left, right)

    chunks(chunk)
    msg_ref[...] = msgf[...].astype(BF16)


def k_second(
    gate_ref, in_ref, x_ref, gsig_ref, slope_ref, win_ref, wout_ref, gin_ref, gout_ref,
    msg_ref, mid_ref, slope_out_ref, *refs
):
    norms0, norms1, gates, facs = refs[:2], refs[2:4], refs[4:6], refs[6:10]
    wide, msgf = refs[10:]
    wide[...] = in_ref[...].astype(F32)

    def chunk(i, b0):
        rows = rows_of(i)
        value = unpack_one(wide, i)
        standard, inv = normalize(value, value.astype(BF16))
        save_norm(norms0, rows, standard, inv)
        update = mm((standard * gout_ref[0:1, :]).astype(BF16), wout_ref[0])
        slope_out_ref[rows, :] = slope_ref[rows, :] * update
        middle = (x_ref[rows, :].astype(F32) + gsig_ref[rows, :] * update).astype(BF16)
        mid_ref[rows, :] = middle
        standard, inv = normalize(middle.astype(F32), middle)
        save_norm(norms1, rows, standard, inv)
        proj = mm((standard * gin_ref[1:2, :]).astype(BF16), win_ref[1])
        left, right = open_gates(gate_ref[rows, :], proj, rows, gates, facs)
        pack_two(msgf, i, left, right)

    chunks(chunk)
    msg_ref[...] = msgf[...].astype(BF16)


def k_third(
    in_ref, mid_ref, gsig_ref, slope_ref, cot_ref, wout_ref, gout_ref,
    msg_ref, out_ref, cot_out_ref, dgate_ref, wide, cotf, outf, msgf, back,
):
    wide[...] = in_ref[...].astype(F32)
    cotf[...] = cot_ref[...].astype(F32)
    back[...] = centered(wout_ref[1], gout_ref[1:2, :])

    def chunk(i, b0):
        rows = rows_of(i)
        grad = load_turned(cotf, b0)
        cot_out_ref[rows, :] = grad.astype(BF16)
        gsig = gsig_ref[rows, :]
        d_update = (grad * gsig).astype(BF16)
        scaled = mm_centered(d_update, back[...])
        value = unpack_one(wide, i)
        standard, inv = normalize(value, value.astype(BF16))
        update = mm((standard * gout_ref[1:2, :]).astype(BF16), wout_ref[1])
        store_turned(outf, b0, mid_ref[rows, :].astype(F32) + gsig * update)
        out_ref[...] = outf[...].astype(BF16)
        dgate_ref[rows, :] = (grad * slope_ref[rows, :] * update).astype(BF16)
        pack_one(msgf, i, norm_back(standard, inv, scaled))

    chunks(chunk)
    send_one(msg_ref, msgf)


def bottom_back(d_left, d_right, dgate_ref, facs, norms, back, rows):
    d_proj = jnp.concatenate(
        [
            (d_left * facs[0][rows, :]).astype(BF16),
            (d_left * facs[1][rows, :]).astype(BF16),
            (d_right * facs[2][rows, :]).astype(BF16),
            (d_right * facs[3][rows, :]).astype(BF16),
            dgate_ref[rows, :],
        ],
        axis=1,
    )
    return norm_back(norms[0][rows, :], norms[1][rows, :], mm_centered(d_proj, back[...]))


def k_fourth(
    in_ref, cot_ref, dgate1_ref, f0, f1, f2, f3, n0, n1, gsig0_ref, slope0_ref, m0, m1,
    win_ref, wout_ref, gin_ref, gout_ref, done_ref, msg_ref, grad_ref, dgate0_ref, far_done_ref,
    wide, msgf, back, out_back, sems,
):
    save = move(done_ref, far_done_ref, sems.at[0])
    wide[...] = in_ref[...].astype(F32)
    back[...] = centered(win_ref[1], gin_ref[1:2, :])
    out_back[...] = centered(wout_ref[0], gout_ref[0:1, :])

    def chunk(i, b0):
        rows = rows_of(i)
        d_left, d_right = unpack_two(wide, i)
        grad = cot_ref[rows, :].astype(F32) + bottom_back(
            d_left, d_right, dgate1_ref, (f0, f1, f2, f3), (n0, n1), back, rows
        )
        grad_ref[rows, :] = grad
        dgate0_ref[rows, :] = (grad * slope0_ref[rows, :]).astype(BF16)
        d_update = (grad * gsig0_ref[rows, :]).astype(BF16)
        scaled = mm_centered(d_update, out_back[...])
        pack_one(msgf, i, norm_back(m0[rows, :], m1[rows, :], scaled))

    chunks(chunk)
    send_one(msg_ref, msgf)
    save.wait()


PIECE = 8


def k_fifth(
    in_ref, grad_ref, dgate0_ref, f0, f1, f2, f3, n0, n1, win_ref, gin_ref, out_ref,
    wide, back, outf, sems,
):
    wide[...] = in_ref[...].astype(F32)
    back[...] = centered(win_ref[0], gin_ref[0:1, :])
    saves = []
    for i in range(B // PIECE):
        rows = rows_of(i, PIECE)
        d_left, d_right = unpack_two(wide, i, PIECE)
        grad = grad_ref[rows, :] + bottom_back(
            d_left, d_right, dgate0_ref, (f0, f1, f2, f3), (n0, n1), back, rows
        )
        for k in range(PIECE):
            outf[pl.ds(i * PIECE + k, A, stride=B), :] = grad[k * A:(k + 1) * A]
        part = pl.ds(i * PIECE, PIECE)
        saves.append(move(outf.reshape(A, B, CH).at[:, part, :], out_ref.at[:, part, :], sems.at[i]))
    for copy in saves:
        copy.wait()


def lanes(n):
    return lax.broadcasted_iota(jnp.int32, (n, 128), 1)


def turn(value, shift):
    shift = shift % 128
    return value if shift == 0 else pltpu.roll(value, shift, axis=1)


def thread(segments, lane):
    value = segments[-1][1]
    for (_, part), (end, _) in zip(reversed(segments[:-1]), reversed(segments[1:])):
        value = jnp.where(lane < end, part, value)
    return value


def inside(t):
    return [p for p in range(8) if p * A < (t + 1) * 128 and (p + 1) * A > t * 128]


def swap(load, n):
    lane = lanes(n)
    turned = []
    for d in range(8):
        tiles = []
        for t in range(3):
            parts = [(max(q * A - t * 128, 0), load((q + d) % 8, t)) for q in inside(t)]
            tiles.append(turn(thread(parts, lane), A * d))
        turned.append(tiles)
    for q in range(8):
        t0, off = divmod(q * A, 128)
        split = min(A, 128 - off)
        result = []
        for t in range(3):
            segments = []
            for p in inside(t):
                base = p * A - t * 128
                pieces = [(0, split, t0)] + ([(split, A, t0 + 1)] if split < A else [])
                for first, last, source in pieces:
                    if base + last > 0 and base + first < 128:
                        segments.append((max(base + first, 0), turned[(p - q) % 8][source]))
            result.append(thread(segments, lane))
        yield q, result


PART = 8


def narrow(tiles, dst):
    for t in range(3):
        dst[:, t * 128:(t + 1) * 128] = tiles[t * RES:(t + 1) * RES, :].astype(BF16)


def keep(tiles, value):
    for t in range(3):
        tiles[t * RES:(t + 1) * RES, :] = value[:, t * 128:(t + 1) * 128]


def join_two(x_ref, xf, lf, rf, lt, rt):
    xf[...] = x_ref[...].astype(F32)
    group = COLS * TWO_ROWS
    for n in range(0, 96, PART):
        def load(r, t):
            return xf[pl.ds(r * group + 3 * n + t, PART, stride=3), :]

        for p, tiles in swap(load, PART):
            dst = (lf, rf)[p % 2]
            for t in range(3):
                dst[pl.ds(t * RES + 4 * n + p // 2, PART, stride=4), :] = tiles[t]
    narrow(lf, lt)
    narrow(rf, rt)


def split_two(lf, rf, o_ref, of):
    group = COLS * TWO_ROWS
    for n in range(0, 96, PART):
        def load(p, t):
            return (lf, rf)[p % 2][pl.ds(t * RES + 4 * n + p // 2, PART, stride=4), :]

        for r, tiles in swap(load, PART):
            for t in range(3):
                of[pl.ds(r * group + 3 * n + t, PART, stride=3), :] = tiles[t]
    o_ref[...] = of[...].astype(BF16)


def join_one(x_ref, xf, df, dst):
    xf[...] = x_ref[...].astype(F32)
    group = COLS * ONE_ROWS
    for m in range(3):
        for c in range(0, COLS, PART):
            def load(r, t):
                return xf[pl.ds(r * group + c * ONE_ROWS + 3 * m + t, PART, stride=ONE_ROWS), :]

            for q, tiles in swap(load, PART):
                for t in range(3):
                    df[pl.ds(t * RES + c * B + 8 * m + q, PART, stride=B), :] = tiles[t]
    narrow(df, dst)


def split_one(value, o_ref, of):
    group = COLS * ONE_ROWS
    for m in range(3):
        for c in range(0, COLS, PART):
            def load(q, t):
                return value[pl.ds(t * RES + c * B + 8 * m + q, PART, stride=B), :]

            for r, tiles in swap(load, PART):
                for t in range(3):
                    of[pl.ds(r * group + c * ONE_ROWS + 3 * m + t, PART, stride=ONE_ROWS), :] = tiles[t]
    send_one(o_ref, of)


def m_forward(u, x_ref, o_ref, lt, rt, xf, lf, rf, prod, of):
    join_two(x_ref, xf, lf, rf, lt, rt)
    if u == 0:
        keep(prod, mm_tn(rt[...], lt[...]))
    else:
        keep(prod, mm_nt(rt[...], lt[...]))
    split_one(prod, o_ref, of)


def m_backward(u, x_ref, lt, rt, o_ref, xf, df, dt, prod_l, prod_r, of):
    join_one(x_ref, xf, df, dt)
    if u == 0:
        keep(prod_l, mm(rt[...], dt[...]))
        keep(prod_r, mm_nt(lt[...], dt[...]))
    else:
        keep(prod_l, mm_tn(dt[...], rt[...]))
        keep(prod_r, mm(dt[...], lt[...]))
    split_two(prod_l, prod_r, o_ref, of)


def shape(*dims, dtype=BF16):
    return jax.ShapeDtypeStruct(dims, dtype)


def call(fn, outs, scratch, name, far=(), far_out=()):
    def run(*args):
        specs = [HB if k in far else VM for k in range(len(args))]
        args = [
            pltpu.with_memory_space_constraint(a, pltpu.HBM) if k in far else a
            for k, a in enumerate(args)
        ]
        return pl.pallas_call(
            fn,
            out_shape=outs,
            in_specs=specs,
            out_specs=[HB if k in far_out else VM for k in range(len(outs))],
            scratch_shapes=scratch,
            compiler_params=pltpu.CompilerParams(vmem_limit_bytes=16 * 1024 * 1024),
            name=name,
        )(*args)

    return run


def exchange(message, rows):
    message = message.reshape(ROWS * COLS, rows // 2, 2, 128)
    return lax.all_to_all(message, AXES, 0, 0, tiled=True).reshape(ROWS * COLS * rows, 128)


TWO = (CH * TWO_ROWS, 128)
ONE = (CH * ONE_ROWS, 128)
PAIR = (PAIRS, CH)
FULL = (RES, RES)
TILED = (3 * RES, 128)
KEEP = shape(*PAIR)
WIDE = shape(*PAIR, dtype=F32)


def wide(dims):
    return pltpu.VMEM(dims, F32)


def body(pair_state, tile_mask, weight_in, weight_out, gain_in, gain_out, cotangent):
    w, wo, gi, go = weight_in, weight_out, gain_in, gain_out
    full = shape(*FULL)
    square = pltpu.VMEM((2 * CH, CH), BF16)
    broad = pltpu.VMEM((2 * CH, 5 * CH), BF16)
    forward = [wide(TWO), wide(TILED), wide(TILED), wide(TILED), wide(ONE)]
    backward = [wide(ONE), wide(TILED), pltpu.VMEM(FULL, BF16), wide(TILED), wide(TILED), wide(TWO)]
    msg, x, gate, gi, go, n0, n1, gsig0, slope0, *fac0 = call(
        k_first, (shape(*TWO), KEEP, WIDE) + (shape(2, CH, dtype=F32),) * 2 + (WIDE,) * 8,
        [pltpu.VMEM(PAIR, BF16), pltpu.VMEM((CH, 5 * CH), BF16), wide((2, CH)), wide((2, CH)),
         wide(PAIR), wide(TWO), pltpu.SMEM((TILES, TILES), jnp.int32), DMA((5,))],
        "first", far=(0, 1, 2, 3, 4),
    )(tile_mask, pair_state.reshape(PAIRS, CH), w, gi, go)
    norm_x = (n0, n1)
    msg = exchange(msg, TWO_ROWS)
    msg, lt0, rt0 = call(
        functools.partial(m_forward, 0), (shape(*ONE), full, full), forward, "product0"
    )(msg)
    msg = exchange(msg, ONE_ROWS)
    msg, middle, slope0, i0, i1, m0, m1, gsig1, slope1, *fac1 = call(
        k_second, (shape(*TWO), KEEP) + (WIDE,) * 11, [wide(ONE), wide(TWO)], "second"
    )(gate, msg, x, gsig0, slope0, w, wo, gi, go)
    msg = exchange(msg, TWO_ROWS)
    msg, lt1, rt1 = call(
        functools.partial(m_forward, 1), (shape(*ONE), full, full), forward, "product1"
    )(msg)
    msg = exchange(msg, ONE_ROWS)
    msg, updated, cot, dgate1 = call(
        k_third, (shape(*ONE), KEEP, KEEP, KEEP),
        [wide(ONE), wide(PAIR), wide(PAIR), wide(ONE), square], "third",
    )(msg, middle, gsig1, slope1, cotangent.reshape(PAIRS, CH), wo, go)
    msg = exchange(msg, ONE_ROWS)
    (msg,) = call(functools.partial(m_backward, 1), (shape(*TWO),), backward, "back1")(msg, lt1, rt1)
    msg = exchange(msg, TWO_ROWS)
    msg, grad, dgate0, updated = call(
        k_fourth, (shape(*ONE), WIDE, KEEP, pltpu.HBM(PAIR, BF16)),
        [wide(TWO), wide(ONE), broad, square, DMA((1,))], "fourth", far_out=(3,),
    )(msg, cot, dgate1, *fac1, m0, m1, gsig0, slope0, i0, i1, w, wo, gi, go, updated)
    msg = exchange(msg, ONE_ROWS)
    (msg,) = call(functools.partial(m_backward, 0), (shape(*TWO),), backward, "back0")(msg, lt0, rt0)
    msg = exchange(msg, TWO_ROWS)
    (pair_grad,) = call(
        k_fifth, (pltpu.HBM((A, B, CH), F32),),
        [wide(TWO), broad, wide(PAIR), DMA((B // PIECE,))], "fifth", far_out=(0,),
    )(msg, grad, dgate0, *fac0, *norm_x, w, gi)
    return updated.reshape(A, B, CH), pair_grad


def solution(mesh):
    return jax.shard_map(
        body,
        mesh=mesh,
        in_specs=(P("row", "col", None), P(), P(), P(), P(), P(), P("row", "col", None)),
        out_specs=(P("row", "col", None), P("row", "col", None)),
        check_vma=False,
    )
```

```python
import functools

import jax
import jax.numpy as jnp
from jax import lax
from jax.experimental import pallas as pl
from jax.experimental.pallas import tpu as pltpu
from jax.sharding import PartitionSpec as P

RES = 384
TILES = 3
TILE = RES // TILES
CH = 128
ROWS = 8
COLS = 16
A = RES // ROWS
B = RES // COLS
PAIRS = A * B
NB = 24
CHUNK = NB * A
F32 = jnp.float32
BF16 = jnp.bfloat16
EPS = 1e-05
AXES = ("row", "col")
VM = pl.BlockSpec(memory_space=pltpu.VMEM)
HB = pl.BlockSpec(memory_space=pltpu.HBM)
DMA = pltpu.SemaphoreType.DMA
TWO_ROWS = 18
ONE_ROWS = 10


def mm(x, w):
    return lax.dot_general(x, w, (((1,), (0,)), ((), ())), preferred_element_type=F32)


def mm_nt(x, w):
    return lax.dot_general(x, w, (((1,), (1,)), ((), ())), preferred_element_type=F32)


def mm_tn(x, w):
    return lax.dot_general(x, w, (((0,), (0,)), ((), ())), preferred_element_type=F32)


def gate_chunk(mask_ref, b0):
    row_first = lax.axis_index("row") * A
    col_first = lax.axis_index("col") * B
    t0 = row_first // TILE
    t1 = jnp.minimum(t0 + 1, TILES - 1)
    low = lax.broadcasted_iota(jnp.int32, (A, CH), 0) < (t0 + 1) * TILE - row_first
    parts = []
    for k in range(NB):
        jt = (col_first + b0 + k) // TILE
        m0 = mask_ref[t0, jt].astype(F32)
        m1 = mask_ref[t1, jt].astype(F32)
        parts.append(jnp.where(low, jnp.full((A, CH), m0, F32), jnp.full((A, CH), m1, F32)))
    return jnp.concatenate(parts, axis=0)


def rows_of(chunk, nb=NB):
    return pl.ds(chunk * nb * A, nb * A)


def load_turned(ref, b0):
    return jnp.concatenate([ref[pl.ds(b0 + k, A, stride=B), :] for k in range(NB)], axis=0)


def store_turned(ref, b0, value):
    for k in range(NB):
        ref[pl.ds(b0 + k, A, stride=B), :] = value[k * A:(k + 1) * A]


def pack_two(ref, i, left, right):
    parts = []
    for k in range(NB):
        parts += [left[k * A:(k + 1) * A], right[k * A:(k + 1) * A]]
    items = jnp.concatenate(parts, axis=0)
    for t in range(NB * 2 * A // 128):
        ref[pl.ds(i * (NB * 2 * A // 128) + t, CH, stride=TWO_ROWS), :] = jnp.transpose(items[t * 128:(t + 1) * 128])


def unpack_two(wide, i, nb=NB):
    blocks = nb * 2 * A // 128
    items = jnp.concatenate(
        [jnp.transpose(wide[pl.ds(i * blocks + t, CH, stride=TWO_ROWS), :]) for t in range(blocks)],
        axis=0,
    )
    lefts = [items[k * 2 * A:k * 2 * A + A] for k in range(nb)]
    rights = [items[k * 2 * A + A:(k + 1) * 2 * A] for k in range(nb)]
    return jnp.concatenate(lefts, axis=0), jnp.concatenate(rights, axis=0)


def pack_one(ref, i, value):
    for t in range(NB * A // 128):
        ref[pl.ds(i * (NB * A // 128) + t, CH, stride=ONE_ROWS), :] = jnp.transpose(value[t * 128:(t + 1) * 128])


def unpack_one(wide, i):
    return jnp.concatenate(
        [jnp.transpose(wide[pl.ds(i * (NB * A // 128) + t, CH, stride=ONE_ROWS), :])
         for t in range(NB * A // 128)], axis=0
    )


def send_one(msg_ref, msgf):
    msgf[pl.ds(ONE_ROWS - 1, CH, stride=ONE_ROWS), :] = jnp.zeros((CH, CH), F32)
    msg_ref[...] = msgf[...].astype(BF16)


def chunks(fn):
    for i in range(B // NB):
        fn(i, i * NB)


def move(src, dst, sem):
    copy = pltpu.make_async_copy(src, dst, sem)
    copy.start()
    return copy


def average():
    return jnp.full((CH, CH), 1.0 / CH, BF16)


def normalize(values, short):
    center = values - mm(short, average())
    inv = lax.rsqrt(jnp.mean(center * center, axis=-1, keepdims=True) + EPS)
    return center * inv, inv


def centered(weight, gain_row):
    gain = jnp.transpose(jnp.broadcast_to(gain_row, (CH, CH)))
    scaled = weight.astype(F32) * jnp.concatenate([gain] * (weight.shape[1] // CH), axis=1)
    scaled = scaled - jnp.mean(scaled, axis=0, keepdims=True)
    high = scaled.astype(BF16)
    return jnp.concatenate([high, (scaled - high.astype(F32)).astype(BF16)], axis=0)


def mm_centered(value, weight):
    both = mm_nt(value, weight)
    return both[:, :CH] + both[:, CH:]


def norm_back(standard, inv, scaled):
    return inv * (scaled - standard * jnp.mean(scaled * standard, axis=-1, keepdims=True))


def save_norm(refs, rows, standard, inv):
    refs[0][rows, :] = standard
    refs[1][rows, :] = jnp.broadcast_to(inv, standard.shape)


def open_gates(gate, proj, rows, gate_refs, fac_refs):
    sides = []
    for k in range(2):
        value = proj[:, 2 * k * CH:(2 * k + 1) * CH]
        sig = jax.nn.sigmoid(proj[:, (2 * k + 1) * CH:(2 * k + 2) * CH])
        factor = gate * sig
        side = factor * value
        fac_refs[2 * k][rows, :] = factor
        fac_refs[2 * k + 1][rows, :] = side * (1.0 - sig)
        sides.append(side)
    sig = jax.nn.sigmoid(proj[:, 4 * CH:])
    factor = gate * sig
    gate_refs[0][rows, :] = factor
    gate_refs[1][rows, :] = factor * (1.0 - sig)
    return sides


def k_first(
    far_mask_ref, pair_ref, win_ref, gin_ref, gout_ref, msg_ref, x_ref, gate_ref, gain_ref, gain_out_ref, *refs
):
    norms, gates, facs = refs[:2], refs[2:4], refs[4:8]
    pair, win, gin, gout, wide, msgf, mask_ref, sems = refs[8:]
    far = ((pair_ref, pair), (win_ref.at[0], win), (gin_ref, gin), (gout_ref, gout), (far_mask_ref, mask_ref))
    loads = [move(src, dst, sems.at[k]) for k, (src, dst) in enumerate(far)]
    loads[0].wait()
    wide[...] = pair[...].astype(F32)
    for copy in loads[1:]:
        copy.wait()
    gain_out_ref[...] = gout[...]
    gain_ref[...] = gin[...]

    def chunk(i, b0):
        rows = rows_of(i)
        x = load_turned(wide, b0)
        short = x.astype(BF16)
        x_ref[rows, :] = short
        standard, inv = normalize(x, short)
        save_norm(norms, rows, standard, inv)
        proj = mm((standard * gin[0:1, :]).astype(BF16), win[...])
        gate = gate_chunk(mask_ref, b0)
        gate_ref[rows, :] = gate
        left, right = open_gates(gate, proj, rows, gates, facs)
        pack_two(msgf, i, left, right)

    chunks(chunk)
    msg_ref[...] = msgf[...].astype(BF16)


def k_second(
    gate_ref, in_ref, x_ref, gsig_ref, slope_ref, win_ref, wout_ref, gin_ref, gout_ref,
    msg_ref, mid_ref, slope_out_ref, *refs
):
    norms0, norms1, gates, facs = refs[:2], refs[2:4], refs[4:6], refs[6:10]
    wide, msgf = refs[10:]
    wide[...] = in_ref[...].astype(F32)

    def chunk(i, b0):
        rows = rows_of(i)
        value = unpack_one(wide, i)
        standard, inv = normalize(value, value.astype(BF16))
        save_norm(norms0, rows, standard, inv)
        update = mm((standard * gout_ref[0:1, :]).astype(BF16), wout_ref[0])
        slope_out_ref[rows, :] = slope_ref[rows, :] * update
        middle = (x_ref[rows, :].astype(F32) + gsig_ref[rows, :] * update).astype(BF16)
        mid_ref[rows, :] = middle
        standard, inv = normalize(middle.astype(F32), middle)
        save_norm(norms1, rows, standard, inv)
        proj = mm((standard * gin_ref[1:2, :]).astype(BF16), win_ref[1])
        left, right = open_gates(gate_ref[rows, :], proj, rows, gates, facs)
        pack_two(msgf, i, left, right)

    chunks(chunk)
    msg_ref[...] = msgf[...].astype(BF16)


def k_third(
    in_ref, mid_ref, gsig_ref, slope_ref, cot_ref, wout_ref, gout_ref,
    msg_ref, out_ref, cot_out_ref, dgate_ref, wide, cotf, outf, msgf, back,
):
    wide[...] = in_ref[...].astype(F32)
    cotf[...] = cot_ref[...].astype(F32)
    back[...] = centered(wout_ref[1], gout_ref[1:2, :])

    def chunk(i, b0):
        rows = rows_of(i)
        grad = load_turned(cotf, b0)
        cot_out_ref[rows, :] = grad.astype(BF16)
        gsig = gsig_ref[rows, :]
        d_update = (grad * gsig).astype(BF16)
        scaled = mm_centered(d_update, back[...])
        value = unpack_one(wide, i)
        standard, inv = normalize(value, value.astype(BF16))
        update = mm((standard * gout_ref[1:2, :]).astype(BF16), wout_ref[1])
        store_turned(outf, b0, mid_ref[rows, :].astype(F32) + gsig * update)
        out_ref[...] = outf[...].astype(BF16)
        dgate_ref[rows, :] = (grad * slope_ref[rows, :] * update).astype(BF16)
        pack_one(msgf, i, norm_back(standard, inv, scaled))

    chunks(chunk)
    send_one(msg_ref, msgf)


def bottom_back(d_left, d_right, dgate_ref, facs, norms, back, rows):
    d_proj = jnp.concatenate(
        [
            (d_left * facs[0][rows, :]).astype(BF16),
            (d_left * facs[1][rows, :]).astype(BF16),
            (d_right * facs[2][rows, :]).astype(BF16),
            (d_right * facs[3][rows, :]).astype(BF16),
            dgate_ref[rows, :],
        ],
        axis=1,
    )
    return norm_back(norms[0][rows, :], norms[1][rows, :], mm_centered(d_proj, back[...]))


def k_fourth(
    in_ref, cot_ref, dgate1_ref, f0, f1, f2, f3, n0, n1, gsig0_ref, slope0_ref, m0, m1,
    win_ref, wout_ref, gin_ref, gout_ref, done_ref, msg_ref, grad_ref, dgate0_ref, far_done_ref,
    wide, msgf, back, out_back, sems,
):
    save = move(done_ref, far_done_ref, sems.at[0])
    wide[...] = in_ref[...].astype(F32)
    back[...] = centered(win_ref[1], gin_ref[1:2, :])
    out_back[...] = centered(wout_ref[0], gout_ref[0:1, :])

    def chunk(i, b0):
        rows = rows_of(i)
        d_left, d_right = unpack_two(wide, i)
        grad = cot_ref[rows, :].astype(F32) + bottom_back(
            d_left, d_right, dgate1_ref, (f0, f1, f2, f3), (n0, n1), back, rows
        )
        grad_ref[rows, :] = grad
        dgate0_ref[rows, :] = (grad * slope0_ref[rows, :]).astype(BF16)
        d_update = (grad * gsig0_ref[rows, :]).astype(BF16)
        scaled = mm_centered(d_update, out_back[...])
        pack_one(msgf, i, norm_back(m0[rows, :], m1[rows, :], scaled))

    chunks(chunk)
    send_one(msg_ref, msgf)
    save.wait()


PIECE = 8


def k_fifth(
    in_ref, grad_ref, dgate0_ref, f0, f1, f2, f3, n0, n1, win_ref, gin_ref, out_ref,
    wide, back, outf, sems,
):
    wide[...] = in_ref[...].astype(F32)
    back[...] = centered(win_ref[0], gin_ref[0:1, :])
    saves = []
    for i in range(B // PIECE):
        rows = rows_of(i, PIECE)
        d_left, d_right = unpack_two(wide, i, PIECE)
        grad = grad_ref[rows, :] + bottom_back(
            d_left, d_right, dgate0_ref, (f0, f1, f2, f3), (n0, n1), back, rows
        )
        for k in range(PIECE):
            outf[pl.ds(i * PIECE + k, A, stride=B), :] = grad[k * A:(k + 1) * A]
        part = pl.ds(i * PIECE, PIECE)
        saves.append(move(outf.reshape(A, B, CH).at[:, part, :], out_ref.at[:, part, :], sems.at[i]))
    for copy in saves:
        copy.wait()


def lanes(n):
    return lax.broadcasted_iota(jnp.int32, (n, 128), 1)


def turn(value, shift):
    shift = shift % 128
    return value if shift == 0 else pltpu.roll(value, shift, axis=1)


def thread(segments, lane):
    value = segments[-1][1]
    for (_, part), (end, _) in zip(reversed(segments[:-1]), reversed(segments[1:])):
        value = jnp.where(lane < end, part, value)
    return value


def inside(t):
    return [p for p in range(8) if p * A < (t + 1) * 128 and (p + 1) * A > t * 128]


def swap(load, n):
    lane = lanes(n)
    turned = []
    for d in range(8):
        tiles = []
        for t in range(3):
            parts = [(max(q * A - t * 128, 0), load((q + d) % 8, t)) for q in inside(t)]
            tiles.append(turn(thread(parts, lane), A * d))
        turned.append(tiles)
    for q in range(8):
        t0, off = divmod(q * A, 128)
        split = min(A, 128 - off)
        result = []
        for t in range(3):
            segments = []
            for p in inside(t):
                base = p * A - t * 128
                pieces = [(0, split, t0)] + ([(split, A, t0 + 1)] if split < A else [])
                for first, last, source in pieces:
                    if base + last > 0 and base + first < 128:
                        segments.append((max(base + first, 0), turned[(p - q) % 8][source]))
            result.append(thread(segments, lane))
        yield q, result


PART = 8


def narrow(tiles, dst):
    for t in range(3):
        dst[:, t * 128:(t + 1) * 128] = tiles[t * RES:(t + 1) * RES, :].astype(BF16)


def keep(tiles, value):
    for t in range(3):
        tiles[t * RES:(t + 1) * RES, :] = value[:, t * 128:(t + 1) * 128]


def join_two(x_ref, xf, lf, rf, lt, rt, grouped):
    xf[...] = x_ref[...].astype(F32)
    group = COLS * TWO_ROWS
    part = 16 if grouped else PART
    for n in range(0, 96, part):
        def load(r, t):
            return xf[pl.ds(r * group + 3 * n + t, part, stride=3), :]

        for p, tiles in swap(load, part):
            for t in range(3):
                if grouped:
                    start = p // 2 * 96 + n
                    (lt, rt)[p % 2][start:start + part, t * 128:(t + 1) * 128] = tiles[t].astype(BF16)
                else:
                    (lf, rf)[p % 2][pl.ds(t * RES + 4 * n + p // 2, part, stride=4), :] = tiles[t]
    if not grouped:
        narrow(lf, lt)
        narrow(rf, rt)


def split_two(lf, rf, o_ref, of, grouped):
    group = COLS * TWO_ROWS
    for n in range(0, 96, PART):
        def load(p, t):
            if grouped:
                return (lf, rf)[p % 2][pl.ds(t * RES + p // 2 * 96 + n, PART), :]
            return (lf, rf)[p % 2][pl.ds(t * RES + 4 * n + p // 2, PART, stride=4), :]

        for r, tiles in swap(load, PART):
            for t in range(3):
                of[pl.ds(r * group + 3 * n + t, PART, stride=3), :] = tiles[t]
    o_ref[...] = of[...].astype(BF16)


def join_one(x_ref, xf, df, dst):
    xf[...] = x_ref[...].astype(F32)
    group = COLS * ONE_ROWS
    for m in range(3):
        for c in range(0, COLS, PART):
            def load(r, t):
                return xf[pl.ds(r * group + c * ONE_ROWS + 3 * m + t, PART, stride=ONE_ROWS), :]

            for q, tiles in swap(load, PART):
                for t in range(3):
                    df[pl.ds(t * RES + c * B + 8 * m + q, PART, stride=B), :] = tiles[t]
    narrow(df, dst)


def split_one(value, o_ref, of):
    group = COLS * ONE_ROWS
    for m in range(3):
        for c in range(0, COLS, PART):
            def load(q, t):
                return value[pl.ds(t * RES + c * B + 8 * m + q, PART, stride=B), :]

            for r, tiles in swap(load, PART):
                for t in range(3):
                    of[pl.ds(r * group + c * ONE_ROWS + 3 * m + t, PART, stride=ONE_ROWS), :] = tiles[t]
    send_one(o_ref, of)


def m_forward(u, x_ref, o_ref, lt, rt, xf, lf, rf, prod, of):
    join_two(x_ref, xf, lf, rf, lt, rt, u == 0)
    if u == 0:
        keep(prod, mm_tn(rt[...], lt[...]))
    else:
        keep(prod, mm_nt(rt[...], lt[...]))
    split_one(prod, o_ref, of)


def m_backward(u, x_ref, lt, rt, o_ref, xf, df, dt, prod_l, prod_r, of):
    join_one(x_ref, xf, df, dt)
    if u == 0:
        keep(prod_l, mm(rt[...], dt[...]))
        keep(prod_r, mm_nt(lt[...], dt[...]))
    else:
        keep(prod_l, mm_tn(dt[...], rt[...]))
        keep(prod_r, mm(dt[...], lt[...]))
    split_two(prod_l, prod_r, o_ref, of, u == 0)


def shape(*dims, dtype=BF16):
    return jax.ShapeDtypeStruct(dims, dtype)


def call(fn, outs, scratch, name, far=(), far_out=()):
    def run(*args):
        specs = [HB if k in far else VM for k in range(len(args))]
        args = [
            pltpu.with_memory_space_constraint(a, pltpu.HBM) if k in far else a
            for k, a in enumerate(args)
        ]
        return pl.pallas_call(
            fn,
            out_shape=outs,
            in_specs=specs,
            out_specs=[HB if k in far_out else VM for k in range(len(outs))],
            scratch_shapes=scratch,
            compiler_params=pltpu.CompilerParams(vmem_limit_bytes=16 * 1024 * 1024),
            name=name,
        )(*args)

    return run


def exchange(message, rows):
    message = message.reshape(ROWS * COLS, rows // 2, 2, 128)
    return lax.all_to_all(message, AXES, 0, 0, tiled=True).reshape(ROWS * COLS * rows, 128)


TWO = (CH * TWO_ROWS, 128)
ONE = (CH * ONE_ROWS, 128)
PAIR = (PAIRS, CH)
FULL = (RES, RES)
TILED = (3 * RES, 128)
KEEP = shape(*PAIR)
WIDE = shape(*PAIR, dtype=F32)


def wide(dims):
    return pltpu.VMEM(dims, F32)


def body(pair_state, tile_mask, weight_in, weight_out, gain_in, gain_out, cotangent):
    w, wo, gi, go = weight_in, weight_out, gain_in, gain_out
    full = shape(*FULL)
    square = pltpu.VMEM((2 * CH, CH), BF16)
    broad = pltpu.VMEM((2 * CH, 5 * CH), BF16)
    forward = [wide(TWO), wide(TILED), wide(TILED), wide(TILED), wide(ONE)]
    backward = [wide(ONE), wide(TILED), pltpu.VMEM(FULL, BF16), wide(TILED), wide(TILED), wide(TWO)]
    msg, x, gate, gi, go, n0, n1, gsig0, slope0, *fac0 = call(
        k_first, (shape(*TWO), KEEP, WIDE) + (shape(2, CH, dtype=F32),) * 2 + (WIDE,) * 8,
        [pltpu.VMEM(PAIR, BF16), pltpu.VMEM((CH, 5 * CH), BF16), wide((2, CH)), wide((2, CH)),
         wide(PAIR), wide(TWO), pltpu.SMEM((TILES, TILES), jnp.int32), DMA((5,))],
        "first", far=(0, 1, 2, 3, 4),
    )(tile_mask, pair_state.reshape(PAIRS, CH), w, gi, go)
    norm_x = (n0, n1)
    msg = exchange(msg, TWO_ROWS)
    msg, lt0, rt0 = call(
        functools.partial(m_forward, 0), (shape(*ONE), full, full), forward, "product0"
    )(msg)
    msg = exchange(msg, ONE_ROWS)
    msg, middle, slope0, i0, i1, m0, m1, gsig1, slope1, *fac1 = call(
        k_second, (shape(*TWO), KEEP) + (WIDE,) * 11, [wide(ONE), wide(TWO)], "second"
    )(gate, msg, x, gsig0, slope0, w, wo, gi, go)
    msg = exchange(msg, TWO_ROWS)
    msg, lt1, rt1 = call(
        functools.partial(m_forward, 1), (shape(*ONE), full, full), forward, "product1"
    )(msg)
    msg = exchange(msg, ONE_ROWS)
    msg, updated, cot, dgate1 = call(
        k_third, (shape(*ONE), KEEP, KEEP, KEEP),
        [wide(ONE), wide(PAIR), wide(PAIR), wide(ONE), square], "third",
    )(msg, middle, gsig1, slope1, cotangent.reshape(PAIRS, CH), wo, go)
    msg = exchange(msg, ONE_ROWS)
    (msg,) = call(functools.partial(m_backward, 1), (shape(*TWO),), backward, "back1")(msg, lt1, rt1)
    msg = exchange(msg, TWO_ROWS)
    msg, grad, dgate0, updated = call(
        k_fourth, (shape(*ONE), WIDE, KEEP, pltpu.HBM(PAIR, BF16)),
        [wide(TWO), wide(ONE), broad, square, DMA((1,))], "fourth", far_out=(3,),
    )(msg, cot, dgate1, *fac1, m0, m1, gsig0, slope0, i0, i1, w, wo, gi, go, updated)
    msg = exchange(msg, ONE_ROWS)
    (msg,) = call(functools.partial(m_backward, 0), (shape(*TWO),), backward, "back0")(msg, lt0, rt0)
    msg = exchange(msg, TWO_ROWS)
    (pair_grad,) = call(
        k_fifth, (pltpu.HBM((A, B, CH), F32),),
        [wide(TWO), broad, wide(PAIR), DMA((B // PIECE,))], "fifth", far_out=(0,),
    )(msg, grad, dgate0, *fac0, *norm_x, w, gi)
    return updated.reshape(A, B, CH), pair_grad


def solution(mesh):
    return jax.shard_map(
        body,
        mesh=mesh,
        in_specs=(P("row", "col", None), P(), P(), P(), P(), P(), P("row", "col", None)),
        out_specs=(P("row", "col", None), P("row", "col", None)),
        check_vma=False,
    )
```
